256 devices in a mesh: gx: 16 (over y_lo, z), gy: 16 (over x, y_hi, core).
Axes of the slice: x: 4, y: 4 (y_hi: 2, y_lo: 2; y = y_hi * 2 + y_lo), z: 8, core: 2. Of those that a mesh axis runs over, the one named last changes fastest.
Arguments:
- tokens: bfloat16 [4, 128, 128, 256], P(None, 'gx', 'gy'), may hold values from -6 to 6
- syndrome: int32 [4, 128, 128], P(None, 'gx', 'gy'), may hold values 0 or 1
- check_plan_step: int32 [4, 128, 128], P(None, 'gx', 'gy'), may hold values from 0 to 7
- offsets: int32 [6, 2], replicated, may hold values from 0 to 8, as said below
- flip_vector: float32 [256], replicated, may hold values from -3 to 3
- plan_step_embedding: float32 [8, 256], replicated, may hold values from -3 to 3
- gain_tanner: float32 [256], replicated, may hold values from 0.5 to 1.5
- w_query: bfloat16 [256, 256], replicated, may hold values from -0.375 to 0.375
- w_key_value: bfloat16 [256, 512], replicated, may hold values from -0.375 to 0.375
- w_merge: bfloat16 [256, 256], replicated, may hold values from -0.375 to 0.375
- gain_time: float32 [256], replicated, may hold values from 0.5 to 1.5
- w_temporal: bfloat16 [256, 768], replicated, may hold values from -0.375 to 0.375
- w_temporal_out: bfloat16 [256, 256], replicated, may hold values from -0.375 to 0.375
- gain_ffn: float32 [256], replicated, may hold values from 0.5 to 1.5
- w_ffn_up: bfloat16 [256, 1024], replicated, may hold values from -0.375 to 0.375
- w_ffn_down: bfloat16 [1024, 256], replicated, may hold values from -0.1875 to 0.1875
- cotangent: bfloat16 [4, 128, 128, 256], P(None, 'gx', 'gy'), may hold values from -6 to 6
Outputs:
- token_grad: bfloat16 [4, 128, 128, 256], P(None, 'gx', 'gy')
- grad_flip: float32 [256], replicated
- plan_step_gradient: float32 [8, 256], replicated
- grad_gain_tanner: float32 [256], replicated
- grad_query: float32 [256, 256], replicated
- grad_key_value: float32 [256, 512], replicated
- grad_merge: float32 [256, 256], replicated
- grad_gain_time: float32 [256], replicated
- grad_temporal: float32 [256, 768], replicated
- grad_temporal_out: float32 [256, 256], replicated
- grad_gain_ffn: float32 [256], replicated
- grad_up: float32 [256, 1024], replicated
- grad_down: float32 [1024, 256], replicated
The draws below stay inside these ranges and needn't reach their ends.
Inputs may be any that keep to these rules, and one draw needn't show every extreme that they name: `offsets`: rows 0, 4 and 5 are (e, 0) and rows 1, 2 and 3 are (0, e), with e from 1 to 8; rows 0 and 3 have e = 8.
All inputs are finite; a program needn't handle non-finite values. No bound on the sum of `syndrome` on one device may be relied on, other than what follows from the above.
Results may differ from the reference program's by a relative error of at most 0.022.
Values may be sent and summed in bfloat16 or wider, within the bound.
A program may use at most 64 MiB of HBM per device.

```python
import math
import jax
import jax.numpy as jnp
from jax import lax

MODEL_WIDTH = 256
HEADS = 8
HEADDIM = 32
FF = 1024
PLAN_STEP_COUNT = 8
MONOS = 6
MAXEXP = 8
SYNDROME_ROUNDS = 4
FIRST_LOOP_SITES = 128
SECOND_LOOP_SITES = 128
TOKENS = 65536


def draw_offsets(key, part):
    powers = jax.random.randint(key, (MONOS,), 1, MAXEXP + 1)
    along_rows = jnp.array([1, 0, 0, 0, 1, 1], dtype=jnp.int32)
    leading = jnp.array([1, 0, 0, 1, 0, 0], dtype=jnp.int32)
    powers = powers * (1 - leading) + MAXEXP * leading
    return jnp.stack([powers * along_rows, powers * (1 - along_rows)], axis=1).astype(jnp.int32)


def with_ends(result, own_key, smallest, high):
    index_at = [jax.random.randint(jax.random.fold_in(own_key, axis), (), 0, length) for axis, length in enumerate(result.shape)]
    main_axis = result.shape.index(max(result.shape))
    next_to = index_at[:main_axis] + [(index_at[main_axis] + 1) % result.shape[main_axis]] + index_at[main_axis + 1:]
    return result.at[tuple(index_at)].set(smallest).at[tuple(next_to)].set(high)


def levels(own_key, extent, shards, smallest, high):
    level, own = 1.0, jax.random.fold_in(own_key, 6)
    for position, parts in shards:
        steps = jnp.exp(jax.random.uniform(jax.random.fold_in(own, position), (parts,), jnp.float32, smallest / len(shards), high / len(shards)))
        level = level * jnp.repeat(steps, extent[position] // parts).reshape([-1 if axis == position else 1 for axis in range(len(extent))])
    return level


def scatter_about(key, dims, scale, reach, shards=(), kind=jnp.bfloat16):
    values = jax.random.normal(key, dims, jnp.float32) * scale
    if len(shards) > 0:
        values = levels(key, dims, shards, -0.22, 0.18) * values
    return jnp.clip(values, min=-reach, max=reach).astype(kind)


def setup_inputs(seed: int = 0) -> dict:
    seeds = jax.random.split(jax.random.key(seed), 18)
    return {
        "tokens": scatter_about(seeds[0], (SYNDROME_ROUNDS, FIRST_LOOP_SITES, SECOND_LOOP_SITES, MODEL_WIDTH), 1.0, 6.0, ((1, 16), (2, 16))),
        "syndrome": with_ends((jax.random.randint(seeds[1], (SYNDROME_ROUNDS, FIRST_LOOP_SITES, SECOND_LOOP_SITES), 0, 4) < 1).astype(jnp.int32), jax.random.fold_in(seeds[1], 1), 0, 1),
        "check_plan_step": with_ends(jax.random.randint(seeds[2], (SYNDROME_ROUNDS, FIRST_LOOP_SITES, SECOND_LOOP_SITES), 0, PLAN_STEP_COUNT), jax.random.fold_in(seeds[2], 1), 0, PLAN_STEP_COUNT - 1).astype(jnp.int32),
        "offsets": draw_offsets(jax.random.fold_in(seeds[17], 71), 0),
        "flip_vector": scatter_about(seeds[4], (MODEL_WIDTH,), 0.5, 3.0, (), jnp.float32),
        "plan_step_embedding": scatter_about(seeds[5], (PLAN_STEP_COUNT, MODEL_WIDTH), 0.5, 3.0, (), jnp.float32),
        "gain_tanner": jnp.clip(1.0 + 0.1 * jax.random.normal(seeds[6], (MODEL_WIDTH,), jnp.float32), 0.5, 1.5),
        "w_query": scatter_about(seeds[7], (MODEL_WIDTH, MODEL_WIDTH), MODEL_WIDTH ** -0.5, 0.375),
        "w_key_value": scatter_about(seeds[8], (MODEL_WIDTH, 2 * MODEL_WIDTH), MODEL_WIDTH ** -0.5, 0.375),
        "w_merge": scatter_about(seeds[9], (MODEL_WIDTH, MODEL_WIDTH), MODEL_WIDTH ** -0.5, 0.375),
        "gain_time": jnp.clip(1.0 + 0.1 * jax.random.normal(seeds[10], (MODEL_WIDTH,), jnp.float32), 0.5, 1.5),
        "w_temporal": scatter_about(seeds[11], (MODEL_WIDTH, 3 * MODEL_WIDTH), MODEL_WIDTH ** -0.5, 0.375),
        "w_temporal_out": scatter_about(seeds[12], (MODEL_WIDTH, MODEL_WIDTH), MODEL_WIDTH ** -0.5, 0.375),
        "gain_ffn": jnp.clip(1.0 + 0.1 * jax.random.normal(seeds[13], (MODEL_WIDTH,), jnp.float32), 0.5, 1.5),
        "w_ffn_up": scatter_about(seeds[14], (MODEL_WIDTH, FF), MODEL_WIDTH ** -0.5, 0.375),
        "w_ffn_down": scatter_about(seeds[15], (FF, MODEL_WIDTH), FF ** -0.5, 0.1875),
        "cotangent": scatter_about(seeds[16], (SYNDROME_ROUNDS, FIRST_LOOP_SITES, SECOND_LOOP_SITES, MODEL_WIDTH), 1.0, 6.0, ((1, 16), (2, 16))),
    }


EPS = 1e-05
CAP = 4.0
EXACT_PRECISION = lax.Precision.HIGHEST

def rms_norm(stream, gain):
    return stream * lax.rsqrt(lax.optimization_barrier(jnp.mean(stream * stream, axis=-1, keepdims=True)) + EPS) * gain

def matmul(inputs, weight):
    return lax.dot_general(inputs, weight, (((inputs.ndim - 1,), (0,)), ((), ())), preferred_element_type=jnp.float32)

def back_matmul(inputs, weight, grad_result):
    grad_low = grad_result.astype(jnp.bfloat16)
    grad_inputs = lax.dot_general(grad_low, weight, (((grad_low.ndim - 1,), (1,)), ((), ())), preferred_element_type=jnp.float32)
    flat_inputs = inputs.reshape(-1, inputs.shape[-1])
    flat_grad = grad_low.reshape(-1, grad_low.shape[-1])
    grad_weight = lax.dot_general(flat_inputs, flat_grad, (((0,), (0,)), ((), ())), preferred_element_type=jnp.float32)
    return (grad_inputs, grad_weight)

def attend(query, moved):
    head_shape = query.shape[:-1] + (HEADS, HEADDIM)
    queries = query.reshape(head_shape)
    weights = []
    for neighbour in moved:
        score = lax.optimization_barrier(jnp.sum(queries * neighbour[..., :MODEL_WIDTH].reshape(head_shape), axis=-1)) / math.sqrt(HEADDIM)
        weights.append(jnp.exp(CAP * jnp.tanh(score / CAP)))
    normalizer = weights[0]
    for weight in weights[1:]:
        normalizer = normalizer + weight
    mixed = jnp.zeros(head_shape, jnp.float32)
    for weight, neighbour in zip(weights, moved):
        mixed = mixed + (weight / normalizer)[..., None] * neighbour[..., MODEL_WIDTH:].reshape(head_shape)
    return mixed.reshape(query.shape)

def tanner_round(query, key_value, offsets):
    moved = [key_value]
    for index in range(MONOS):
        rolled = jnp.roll(key_value, -offsets[index, 0], axis=0)
        moved.append(jnp.roll(rolled, -offsets[index, 1], axis=1))
    return attend(query, moved)

def time_attend(packed):
    head_shape = packed.shape[:-1] + (HEADS, HEADDIM)
    queries = packed[..., :MODEL_WIDTH].reshape(head_shape)
    keys = packed[..., MODEL_WIDTH:2 * MODEL_WIDTH].reshape(head_shape)
    values = packed[..., 2 * MODEL_WIDTH:].reshape(head_shape)
    scores = jnp.einsum('rxyhe,sxyhe->xyhrs', queries, keys, precision=EXACT_PRECISION) / math.sqrt(HEADDIM)
    capped = CAP * jnp.tanh(scores / CAP)
    rounds = packed.shape[0]
    later = lax.broadcasted_iota(jnp.int32, (rounds, rounds), 0)
    earlier = lax.broadcasted_iota(jnp.int32, (rounds, rounds), 1)
    weights = jnp.where(earlier <= later, jnp.exp(capped), 0.0)
    probs = weights / lax.optimization_barrier(jnp.sum(weights, axis=-1, keepdims=True))
    mixed = jnp.einsum('xyhrs,sxyhe->rxyhe', probs, values, precision=EXACT_PRECISION)
    return mixed.reshape(packed.shape[:-1] + (MODEL_WIDTH,))

def reference(tokens, syndrome, check_plan_step, offsets, flip_vector, plan_step_embedding, gain_tanner, w_query, w_key_value, w_merge, gain_time, w_temporal, w_temporal_out, gain_ffn, w_ffn_up, w_ffn_down, cotangent):
    plan_step_onehot = (check_plan_step[..., None] == jnp.arange(PLAN_STEP_COUNT, dtype=jnp.int32)).astype(jnp.float32)
    syndrome_float = syndrome.astype(jnp.float32)
    embedded = tokens.astype(jnp.float32) + syndrome_float[..., None] * flip_vector + jnp.dot(plan_step_onehot, plan_step_embedding, precision=EXACT_PRECISION)
    normed_one, norm_one_back = jax.vjp(rms_norm, embedded, gain_tanner)
    hidden_one = normed_one.astype(jnp.bfloat16)
    query = matmul(hidden_one, w_query).astype(jnp.bfloat16)
    key_value = matmul(hidden_one, w_key_value).astype(jnp.bfloat16)

    def tanner_forward(items):
        return tanner_round(items[0].astype(jnp.float32), items[1].astype(jnp.float32), offsets).astype(jnp.bfloat16)
    mixed_one = lax.map(tanner_forward, (query, key_value))
    after_tanner = embedded + matmul(mixed_one, w_merge)
    normed_two, norm_two_back = jax.vjp(rms_norm, after_tanner, gain_time)
    hidden_two = normed_two.astype(jnp.bfloat16)
    packed = matmul(hidden_two, w_temporal).astype(jnp.bfloat16)
    packed_rows = jnp.moveaxis(packed, 1, 0)

    def time_forward(item):
        return time_attend(item[:, None].astype(jnp.float32))[:, 0].astype(jnp.bfloat16)
    mixed_two = jnp.moveaxis(lax.map(time_forward, packed_rows), 0, 1)
    after_time = after_tanner + matmul(mixed_two, w_temporal_out)

    def ffn_round(items):
        stream, outer = items
        normed_three, norm_three_back = jax.vjp(rms_norm, stream, gain_ffn)
        hidden_three = normed_three.astype(jnp.bfloat16)
        before_act = matmul(hidden_three, w_ffn_up)
        activated, gelu_back = jax.vjp(jax.nn.gelu, before_act)
        activated = activated.astype(jnp.bfloat16)
        grad_output = outer.astype(jnp.float32)
        grad_act, grad_down = back_matmul(activated, w_ffn_down, grad_output)
        grad_before = gelu_back(grad_act)[0]
        grad_three, grad_up = back_matmul(hidden_three, w_ffn_up, grad_before)
        grad_norm, grad_gain = norm_three_back(grad_three)
        return (grad_output + grad_norm, grad_up, grad_down, grad_gain)
    grad_after_time, grad_up, grad_down, grad_gain_ffn = lax.map(ffn_round, (after_time, cotangent))
    grad_up = lax.optimization_barrier(jnp.sum(grad_up, axis=0))
    grad_down = lax.optimization_barrier(jnp.sum(grad_down, axis=0))
    grad_gain_ffn = lax.optimization_barrier(jnp.sum(grad_gain_ffn, axis=0))
    grad_mixed_two, grad_temporal_out = back_matmul(mixed_two, w_temporal_out, grad_after_time)

    def time_grads(items):
        rows_packed, rows_grad = items
        back = jax.vjp(time_attend, rows_packed[:, None].astype(jnp.float32))[1]
        return back(rows_grad[:, None])[0][:, 0]
    grad_packed = jnp.moveaxis(lax.map(time_grads, (packed_rows, jnp.moveaxis(grad_mixed_two, 1, 0))), 0, 1)
    grad_two, grad_temporal = back_matmul(hidden_two, w_temporal, grad_packed)
    grad_norm_two, grad_gain_time = norm_two_back(grad_two)
    grad_after_tanner = grad_after_time + grad_norm_two
    grad_mixed_one, grad_merge = back_matmul(mixed_one, w_merge, grad_after_tanner)

    def tanner_grads(items):
        query_round, key_round, grad_round = items

        def tanner_fixed(query_in, key_in):
            return tanner_round(query_in, key_in, offsets)
        back = jax.vjp(tanner_fixed, query_round.astype(jnp.float32), key_round.astype(jnp.float32))[1]
        return back(grad_round)
    grad_query_out, grad_key_out = lax.map(tanner_grads, (query, key_value, grad_mixed_one))
    grad_one_query, grad_query = back_matmul(hidden_one, w_query, grad_query_out)
    grad_one_key, grad_key_value = back_matmul(hidden_one, w_key_value, grad_key_out)
    grad_norm_one, grad_gain_tanner = norm_one_back(grad_one_query + grad_one_key)
    embedding_gradient = grad_after_tanner + grad_norm_one
    token_grad = embedding_gradient.astype(jnp.bfloat16)
    grad_flip = lax.optimization_barrier(jnp.sum(syndrome_float[..., None] * embedding_gradient, axis=(0, 1, 2)))
    plan_step_gradient = lax.dot_general(plan_step_onehot.reshape(-1, PLAN_STEP_COUNT), embedding_gradient.reshape(-1, MODEL_WIDTH), (((0,), (0,)), ((), ())), precision=EXACT_PRECISION)
    scale = 1.0 / math.sqrt(TOKENS)
    return (token_grad, grad_flip * scale, plan_step_gradient * scale, grad_gain_tanner * scale, grad_query * scale, grad_key_value * scale, grad_merge * scale, grad_gain_time * scale, grad_temporal * scale, grad_temporal_out * scale, grad_gain_ffn * scale, grad_up * scale, grad_down * scale)
```

```python
import math

import jax
import jax.numpy as jnp
from jax import lax
from jax.experimental import pallas as pl
from jax.experimental.pallas import tpu as pltpu
from jax.sharding import PartitionSpec as P

MODEL_WIDTH = 256
HEADDIM = 32
PLAN_STEP_COUNT = 8
MONOS = 6
MAXEXP = 8


EPS = 1e-05
CAP = 4.0
EXACT_PRECISION = lax.Precision.HIGHEST
ALONG_ROWS = (0, 4, 5)


MESH = pl.DeviceIdType.MESH
GROUP_ROWS = 4096
HALF = 2048
SMALL_ROWS = 16


class Place:
    def __init__(self):
        self.gx = lax.axis_index("gx")
        self.gy = lax.axis_index("gy")
        self.z = lax.rem(self.gx, 8)
        self.y_lo = lax.div(self.gx, 8)
        self.core = lax.rem(self.gy, 2)
        self.y_hi = lax.rem(lax.div(self.gy, 2), 2)
        self.x = lax.div(self.gy, 4)
        self.y = self.y_hi * 2 + self.y_lo

    def other_core(self):
        return (self.gx, self.gy + 1 - 2 * self.core)

    def at_x(self, x):
        return (self.gx, x * 4 + self.y_hi * 2 + self.core)

    def at_y(self, y):
        return (lax.rem(y, 2) * 8 + self.z, self.x * 4 + lax.div(y, 2) * 2 + self.core)

    def at_z(self, z):
        return (self.y_lo * 8 + z, self.gy)

    def greeted(self):
        peers = [self.other_core()]
        for step in range(1, 4):
            peers.append(self.at_x(lax.rem(self.x + step, 4)))
            peers.append(self.at_y(lax.rem(self.y + step, 4)))
        for step in range(1, 8):
            peers.append(self.at_z(lax.rem(self.z + step, 8)))
        return peers


def greet(peers):
    barrier = pltpu.get_barrier_semaphore()
    for peer in peers:
        pl.semaphore_signal(barrier, inc=1, device_id=peer, device_id_type=MESH)
    return barrier, len(peers)


def rows(start, count):
    return pl.ds(pl.multiple_of(start, 16), count)


class Sum:
    SCRATCH = (
        pltpu.VMEM((HALF, 128), jnp.bfloat16),
        pltpu.VMEM((HALF, 128), jnp.bfloat16),
        pltpu.VMEM((6, 256, 128), jnp.bfloat16),
        pltpu.VMEM((2, 256, 128), jnp.bfloat16),
        pltpu.VMEM((6, 64, 128), jnp.bfloat16),
        pltpu.VMEM((128, 128), jnp.bfloat16),
        pltpu.VMEM((7, 16, 128), jnp.bfloat16),
        pltpu.SemaphoreType.DMA((40,)),
        pltpu.SemaphoreType.DMA((40,)),
    )

    def __init__(self, place, group, source, result, scratch):
        self.place = place
        self.source = source
        self.base = group * GROUP_ROWS
        self.result = result
        (self.from_core, self.one, self.in_two, self.two, self.in_three, self.three, self.in_four,
         self.send, self.recv) = scratch

    def copy(self, slot, source, target, peer):
        copy = pltpu.make_async_remote_copy(
            src_ref=source,
            dst_ref=target,
            send_sem=self.send.at[slot],
            recv_sem=self.recv.at[slot],
            device_id=peer,
            device_id_type=MESH,
        )
        copy.start()
        return copy

    def core_out(self):
        other = rows((1 - self.place.core) * HALF, HALF)
        self.core_copy = self.copy(0, self.source.at[other], self.from_core, self.place.other_core())

    def core_in(self):
        p = self.place
        self.core_copy.wait()
        own = self.source[rows(p.core * HALF, HALF)]
        self.one[...] = (own.astype(jnp.float32) + self.from_core[...].astype(jnp.float32)).astype(jnp.bfloat16)
        self.copies = []
        for step in range(1, 4):
            x, y = lax.rem(p.x + step, 4), lax.rem(p.y + step, 4)
            self.copies.append(
                self.copy(step, self.one.at[rows(x * 256, 256)], self.in_two.at[step - 1], p.at_x(x)))
            self.copies.append(
                self.copy(3 + step, self.one.at[rows(1024 + y * 256, 256)], self.in_two.at[2 + step], p.at_y(y)))

    def two_in(self):
        p = self.place
        for copy in self.copies:
            copy.wait()
        for part, own in ((0, p.x * 256), (1, 1024 + p.y * 256)):
            total = self.one[rows(own, 256)].astype(jnp.float32)
            for step in range(3):
                total = total + self.in_two[part * 3 + step].astype(jnp.float32)
            self.two[part] = total.astype(jnp.bfloat16)
        self.copies = []
        for step in range(1, 4):
            x, y = lax.rem(p.x + step, 4), lax.rem(p.y + step, 4)
            self.copies.append(
                self.copy(6 + step, self.two.at[0, rows(y * 64, 64)], self.in_three.at[step - 1], p.at_y(y)))
            self.copies.append(
                self.copy(9 + step, self.two.at[1, rows(x * 64, 64)], self.in_three.at[2 + step], p.at_x(x)))

    def three_in(self):
        p = self.place
        for copy in self.copies:
            copy.wait()
        for part, own in ((0, p.y * 64), (1, p.x * 64)):
            total = self.two[part, rows(own, 64)].astype(jnp.float32)
            for step in range(3):
                total = total + self.in_three[part * 3 + step].astype(jnp.float32)
            self.three[part * 64 : part * 64 + 64] = total.astype(jnp.bfloat16)
        self.copies = []
        for step in range(1, 8):
            z = lax.rem(p.z + step, 8)
            self.copies.append(
                self.copy(12 + step, self.three.at[rows(z * 16, 16)], self.in_four.at[step - 1], p.at_z(z)))

    def four_in(self):
        p = self.place
        for copy in self.copies:
            copy.wait()
        total = self.three[rows(p.z * 16, 16)].astype(jnp.float32)
        for step in range(7):
            total = total + self.in_four[step].astype(jnp.float32)
        half = self.base + p.core * HALF
        self.first = half + p.x * 256 + p.y * 64
        self.second = half + 1024 + p.y * 256 + p.x * 64
        upper = lax.div(p.z, 4)
        own = (1 - upper) * self.first + upper * self.second + lax.rem(p.z, 4) * 16
        self.result[rows(own, 16)] = total.astype(jnp.bfloat16)
        self.copies = []
        for step in range(1, 8):
            z = lax.rem(p.z + step, 8)
            tile = self.result.at[rows(own, 16)]
            self.copies.append(self.copy(19 + step, tile, tile, p.at_z(z)))

    def z_gathered(self):
        p = self.place
        for copy in self.copies:
            copy.wait()
        first, second = self.result.at[rows(self.first, 64)], self.result.at[rows(self.second, 64)]
        self.copies = []
        for step in range(1, 4):
            x, y = lax.rem(p.x + step, 4), lax.rem(p.y + step, 4)
            self.copies.append(self.copy(26 + step, first, first, p.at_y(y)))
            self.copies.append(self.copy(29 + step, second, second, p.at_x(x)))

    def one_gathered(self):
        p = self.place
        for copy in self.copies:
            copy.wait()
        half = self.base + p.core * HALF
        first = self.result.at[rows(half + p.x * 256, 256)]
        second = self.result.at[rows(half + 1024 + p.y * 256, 256)]
        self.copies = []
        for step in range(1, 4):
            x, y = lax.rem(p.x + step, 4), lax.rem(p.y + step, 4)
            self.copies.append(self.copy(32 + step, first, first, p.at_x(x)))
            self.copies.append(self.copy(35 + step, second, second, p.at_y(y)))

    def both_gathered(self):
        p = self.place
        for copy in self.copies:
            copy.wait()
        own = self.result.at[rows(self.base + p.core * HALF, HALF)]
        self.core_copy = self.copy(39, own, own, p.other_core())

    def finish(self):
        self.core_copy.wait()


class SmallSum:
    SCRATCH = (
        pltpu.VMEM((2, SMALL_ROWS, 256), jnp.float32),
        pltpu.VMEM((4, SMALL_ROWS, 256), jnp.float32),
        pltpu.VMEM((4, SMALL_ROWS, 256), jnp.float32),
        pltpu.VMEM((8, SMALL_ROWS, 256), jnp.float32),
        pltpu.SemaphoreType.DMA((14,)),
        pltpu.SemaphoreType.DMA((14,)),
    )

    def __init__(self, place, scratch):
        self.place = place
        self.slots = scratch[:4]
        self.send, self.recv = scratch[4:]
        self.stage = -1

    def out(self, value):
        p = self.place
        self.stage += 1
        slots = self.slots[self.stage]
        mine = (p.core, p.x, p.y, p.z)[self.stage]
        at = (lambda _: p.other_core(), p.at_x, p.at_y, p.at_z)[self.stage]
        first = (0, 1, 4, 7)[self.stage]
        count = slots.shape[0]
        slots[mine] = value
        self.copies = []
        for step in range(1, count):
            copy = pltpu.make_async_remote_copy(
                src_ref=slots.at[mine],
                dst_ref=slots.at[mine],
                send_sem=self.send.at[first + step - 1],
                recv_sem=self.recv.at[first + step - 1],
                device_id=at(lax.rem(mine + step, count)),
                device_id_type=MESH,
            )
            copy.start()
            self.copies.append(copy)

    def total(self):
        for copy in self.copies:
            copy.wait()
        slots = self.slots[self.stage]
        total = slots[0]
        for index in range(1, slots.shape[0]):
            total = total + slots[index]
        return total


def sum_kernel(early_ref, late_ref, small_ref, result_ref, small_result_ref, *scratch):
    place = Place()
    barrier, count = greet(place.greeted())
    pl.semaphore_wait(barrier, count)
    per = len(Sum.SCRATCH)
    early = Sum(place, 0, early_ref, result_ref, scratch[:per])
    late = Sum(place, 1, late_ref, result_ref, scratch[per : 2 * per])
    small = SmallSum(place, scratch[2 * per :])
    early.core_out()
    late.core_out()
    small.out(small_ref[...])
    early.core_in()
    late.core_in()
    small.out(small.total())
    early.two_in()
    late.two_in()
    small.out(small.total())
    early.three_in()
    late.three_in()
    small.out(small.total())
    early.four_in()
    late.four_in()
    small_result_ref[...] = small.total()
    early.z_gathered()
    late.z_gathered()
    early.one_gathered()
    late.one_gathered()
    early.both_gathered()
    late.both_gathered()
    early.finish()
    late.finish()


def sum_everywhere(early, late, small):
    vmem = pl.BlockSpec(memory_space=pltpu.VMEM)
    return pl.pallas_call(
        sum_kernel,
        out_shape=(
            jax.ShapeDtypeStruct((2 * GROUP_ROWS, 128), jnp.bfloat16),
            jax.ShapeDtypeStruct((SMALL_ROWS, 256), jnp.float32),
        ),
        in_specs=[vmem] * 3,
        out_specs=(vmem, vmem),
        scratch_shapes=list(Sum.SCRATCH + Sum.SCRATCH + SmallSum.SCRATCH),
        compiler_params=pltpu.CompilerParams(
            collective_id=0, has_side_effects=True, vmem_limit_bytes=40 * 2**20),
    )(early, late, small)


def to_slabs(*grads):
    slabs = []
    for grad in grads:
        blocks, columns = grad.shape[0] // 256, grad.shape[1] // 128
        slabs.append(grad.reshape(blocks, 256, columns, 128).transpose(0, 2, 1, 3).reshape(-1, 128))
    return jnp.concatenate(slabs).astype(jnp.bfloat16)


def from_slabs(slabs, scale, *shapes):
    grads, at = [], 0
    for depth, width in shapes:
        count = depth * width // 128
        piece = slabs[at : at + count].reshape(depth // 256, width // 128, 256, 128).transpose(0, 2, 1, 3)
        grads.append(piece.reshape(depth, width).astype(jnp.float32) * scale)
        at += count
    return grads


def shifted(x, axis, by):
    count = lax.axis_size(axis)
    return lax.ppermute(x, axis, [(i, (i + by) % count) for i in range(count)])


def rms_norm(stream, gain):
    return stream * lax.rsqrt(jnp.mean(stream * stream, axis=-1, keepdims=True) + EPS) * gain


def matmul(inputs, weight):
    return lax.dot_general(
        inputs, weight, (((inputs.ndim - 1,), (0,)), ((), ())), preferred_element_type=jnp.float32
    )


def back_matmul(inputs, weight, grad_result):
    grad_low = grad_result.astype(jnp.bfloat16)
    grad_inputs = lax.dot_general(
        grad_low,
        weight,
        (((grad_low.ndim - 1,), (1,)), ((), ())),
        preferred_element_type=jnp.float32,
    )
    flat_inputs = inputs.reshape(-1, inputs.shape[-1])
    flat_grad = grad_low.reshape(-1, grad_low.shape[-1])
    grad_weight = lax.dot_general(
        flat_inputs, flat_grad, (((0,), (0,)), ((), ())), preferred_element_type=jnp.float32
    )
    return (grad_inputs, grad_weight)


def head_total(product):
    width = product.shape[-1]
    row_head = lax.broadcasted_iota(jnp.int32, (width, width), 0) // HEADDIM
    col_head = lax.broadcasted_iota(jnp.int32, (width, width), 1) // HEADDIM
    block = (row_head == col_head).astype(jnp.float32)
    return lax.dot_general(
        product, block, (((product.ndim - 1,), (0,)), ((), ())), precision=EXACT_PRECISION
    )


def attend(query, moved):
    weights = []
    for neighbour in moved:
        score = head_total(query * neighbour[..., :MODEL_WIDTH]) / math.sqrt(HEADDIM)
        weights.append(jnp.exp(CAP * jnp.tanh(score / CAP)))
    normalizer = weights[0]
    for weight in weights[1:]:
        normalizer = normalizer + weight
    mixed = jnp.zeros(query.shape, jnp.float32)
    for weight, neighbour in zip(weights, moved):
        mixed = mixed + weight / normalizer * neighbour[..., MODEL_WIDTH:]
    return mixed


def tanner_local(query, key_value, next_rows, next_cols, offsets):
    extended_rows = jnp.concatenate([key_value, next_rows], axis=1)
    extended_cols = jnp.concatenate([key_value, next_cols], axis=2)
    moved = [key_value]
    for index in range(MONOS):
        if index in ALONG_ROWS:
            moved.append(
                lax.dynamic_slice_in_dim(extended_rows, offsets[index, 0], key_value.shape[1], 1)
            )
        else:
            moved.append(
                lax.dynamic_slice_in_dim(extended_cols, offsets[index, 1], key_value.shape[2], 2)
            )
    return attend(query, moved)


def time_attend(packed):
    queries = packed[..., :MODEL_WIDTH]
    keys = packed[..., MODEL_WIDTH : 2 * MODEL_WIDTH]
    values = packed[..., 2 * MODEL_WIDTH :]
    outputs = []
    for later in range(packed.shape[0]):
        weights = []
        for earlier in range(later + 1):
            score = head_total(queries[later] * keys[earlier]) / math.sqrt(HEADDIM)
            weights.append(jnp.exp(CAP * jnp.tanh(score / CAP)))
        normalizer = weights[0]
        for weight in weights[1:]:
            normalizer = normalizer + weight
        mixed = jnp.zeros(queries.shape[1:], jnp.float32)
        for earlier in range(later + 1):
            mixed = mixed + weights[earlier] / normalizer * values[earlier]
        outputs.append(mixed)
    return jnp.stack(outputs, axis=0)


def on_device(
    tokens,
    syndrome,
    check_plan_step,
    offsets,
    flip_vector,
    plan_step_embedding,
    gain_tanner,
    w_query,
    w_key_value,
    w_merge,
    gain_time,
    w_temporal,
    w_temporal_out,
    gain_ffn,
    w_ffn_up,
    w_ffn_down,
    cotangent,
):
    plan_step_onehot = (
        check_plan_step[..., None] == jnp.arange(PLAN_STEP_COUNT, dtype=jnp.int32)
    ).astype(jnp.float32)
    syndrome_float = syndrome.astype(jnp.float32)
    embedded = (
        tokens.astype(jnp.float32)
        + syndrome_float[..., None] * flip_vector
        + jnp.dot(plan_step_onehot, plan_step_embedding, precision=EXACT_PRECISION)
    )
    normed_one, norm_one_back = jax.vjp(rms_norm, embedded, gain_tanner)
    hidden_one = normed_one.astype(jnp.bfloat16)
    query = matmul(hidden_one, w_query).astype(jnp.bfloat16)
    key_value = matmul(hidden_one, w_key_value).astype(jnp.bfloat16)
    next_rows = shifted(key_value, "gx", -1)
    next_cols = shifted(key_value, "gy", -1)

    def tanner_part(query_in, key_in, rows_in, cols_in):
        return tanner_local(query_in, key_in, rows_in, cols_in, offsets)

    mixed_float, tanner_back = jax.vjp(
        tanner_part,
        query.astype(jnp.float32),
        key_value.astype(jnp.float32),
        next_rows.astype(jnp.float32),
        next_cols.astype(jnp.float32),
    )
    mixed_one = mixed_float.astype(jnp.bfloat16)
    after_tanner = embedded + matmul(mixed_one, w_merge)
    normed_two, norm_two_back = jax.vjp(rms_norm, after_tanner, gain_time)
    hidden_two = normed_two.astype(jnp.bfloat16)
    packed = matmul(hidden_two, w_temporal).astype(jnp.bfloat16)
    mixed_time, time_back = jax.vjp(time_attend, packed.astype(jnp.float32))
    mixed_two = mixed_time.astype(jnp.bfloat16)
    after_time = after_tanner + matmul(mixed_two, w_temporal_out)
    normed_three, norm_three_back = jax.vjp(rms_norm, after_time, gain_ffn)
    hidden_three = normed_three.astype(jnp.bfloat16)
    before_act = matmul(hidden_three, w_ffn_up)
    activated_float, gelu_back = jax.vjp(jax.nn.gelu, before_act)
    activated = activated_float.astype(jnp.bfloat16)
    grad_output = cotangent.astype(jnp.float32)
    grad_act, grad_down = back_matmul(activated, w_ffn_down, grad_output)
    grad_before = gelu_back(grad_act)[0]
    grad_three, grad_up = back_matmul(hidden_three, w_ffn_up, grad_before)
    grad_norm_three, grad_gain_ffn = norm_three_back(grad_three)
    grad_after_time = grad_output + grad_norm_three
    grad_mixed_two, grad_temporal_out = back_matmul(mixed_two, w_temporal_out, grad_after_time)
    grad_packed = time_back(grad_mixed_two)[0]
    grad_two, grad_temporal = back_matmul(hidden_two, w_temporal, grad_packed)
    grad_norm_two, grad_gain_time = norm_two_back(grad_two)
    grad_after_tanner = grad_after_time + grad_norm_two
    scale = 1.0 / math.sqrt(
        tokens.shape[0]
        * tokens.shape[1]
        * tokens.shape[2]
        * lax.axis_size("gx")
        * lax.axis_size("gy")
    )
    grad_mixed_one, grad_merge = back_matmul(mixed_one, w_merge, grad_after_tanner)
    grad_query_out, grad_key_local, grad_rows, grad_cols = tanner_back(grad_mixed_one)
    back_rows = shifted(grad_rows.astype(jnp.bfloat16), "gx", 1).astype(grad_rows.dtype)
    back_cols = shifted(grad_cols.astype(jnp.bfloat16), "gy", 1).astype(grad_cols.dtype)
    grad_key_out = grad_key_local.at[:, :MAXEXP].add(back_rows)
    grad_key_out = grad_key_out.at[:, :, :MAXEXP].add(back_cols)
    grad_one_key, grad_key_value = back_matmul(hidden_one, w_key_value, grad_key_out)
    grad_one_query, grad_query = back_matmul(hidden_one, w_query, grad_query_out)
    grad_norm_one, grad_gain_tanner = norm_one_back(grad_one_query + grad_one_key)
    embedding_gradient = grad_after_tanner + grad_norm_one
    token_grad = embedding_gradient.astype(jnp.bfloat16)
    grad_flip = jnp.sum(syndrome_float[..., None] * embedding_gradient, axis=(0, 1, 2))
    plan_step_gradient = lax.dot_general(
        plan_step_onehot.reshape(-1, PLAN_STEP_COUNT),
        embedding_gradient.reshape(-1, MODEL_WIDTH),
        (((0,), (0,)), ((), ())),
        precision=EXACT_PRECISION,
    )
    small = jnp.concatenate(
        [
            grad_flip[None],
            plan_step_gradient,
            grad_gain_tanner[None],
            grad_gain_time[None],
            grad_gain_ffn[None],
            jnp.zeros((SMALL_ROWS - 12, MODEL_WIDTH), jnp.float32),
        ]
    )
    early = to_slabs(grad_down, grad_up)
    late = to_slabs(grad_query, grad_key_value, grad_merge, grad_temporal, grad_temporal_out)
    slabs, small = sum_everywhere(early, late, small)
    down, up, query_g, key_value_g, merge_g, temporal_g, temporal_out_g = from_slabs(
        slabs,
        scale,
        (1024, 256),
        (256, 1024),
        (256, 256),
        (256, 512),
        (256, 256),
        (256, 768),
        (256, 256),
    )
    small = small * scale
    return (
        token_grad,
        small[0],
        small[1:9],
        small[9],
        query_g,
        key_value_g,
        merge_g,
        small[10],
        temporal_g,
        temporal_out_g,
        small[11],
        up,
        down,
    )


def solution(mesh):
    return jax.shard_map(
        on_device,
        mesh=mesh,
        in_specs=(
            P(None, "gx", "gy", None),
            P(None, "gx", "gy"),
            P(None, "gx", "gy"),
            P(),
            P(),
            P(),
            P(),
            P(),
            P(),
            P(),
            P(),
            P(),
            P(),
            P(),
            P(),
            P(),
            P(None, "gx", "gy", None),
        ),
        out_specs=(
            P(None, "gx", "gy", None),
            P(),
            P(),
            P(),
            P(),
            P(),
            P(),
            P(),
            P(),
            P(),
            P(),
            P(),
            P(),
        ),
        check_vma=False,
    )
```

```python
import math

import jax
import jax.numpy as jnp
from jax import lax
from jax.experimental import pallas as pl
from jax.experimental.pallas import tpu as pltpu
from jax.sharding import PartitionSpec as P

WIDTH = 256
HEADDIM = 32
FF = 1024
PLAN_STEP_COUNT = 8
TOKENS = 256
NEIGHBOURS = 7
ROUNDS = 4
EPS = 1e-05
CAP = 4.0
ROOT = math.sqrt(HEADDIM)
GELU = math.sqrt(2 / math.pi)

MESH = pl.DeviceIdType.MESH
GROUP_ROWS = 4096
HALF = 2048
SMALL_ROWS = 16


class Place:
    def __init__(self):
        self.gx = lax.axis_index("gx")
        self.gy = lax.axis_index("gy")
        self.z = lax.rem(self.gx, 8)
        self.y_lo = lax.div(self.gx, 8)
        self.core = lax.rem(self.gy, 2)
        self.y_hi = lax.rem(lax.div(self.gy, 2), 2)
        self.x = lax.div(self.gy, 4)
        self.y = self.y_hi * 2 + self.y_lo

    def other_core(self):
        return (self.gx, self.gy + 1 - 2 * self.core)

    def at_x(self, x):
        return (self.gx, x * 4 + self.y_hi * 2 + self.core)

    def at_y(self, y):
        return (lax.rem(y, 2) * 8 + self.z, self.x * 4 + lax.div(y, 2) * 2 + self.core)

    def at_z(self, z):
        return (self.y_lo * 8 + z, self.gy)

    def greeted(self):
        peers = [self.other_core()]
        for step in range(1, 4):
            peers.append(self.at_x(lax.rem(self.x + step, 4)))
            peers.append(self.at_y(lax.rem(self.y + step, 4)))
        for step in range(1, 8):
            peers.append(self.at_z(lax.rem(self.z + step, 8)))
        for step in (1, 15):
            peers.append(self.row_tile(step))
            peers.append(self.column_tile(step))
        return peers

    def row_tile(self, step):
        return (lax.rem(self.gx + step, 16), self.gy)

    def column_tile(self, step):
        return (self.gx, lax.rem(self.gy + step, 16))


def greet(peers):
    barrier = pltpu.get_barrier_semaphore()
    for peer in peers:
        pl.semaphore_signal(barrier, inc=1, device_id=peer, device_id_type=MESH)
    return barrier, len(peers)


def rows(start, count):
    return pl.ds(pl.multiple_of(start, 16), count)


class Sum:
    SCRATCH = (
        pltpu.VMEM((HALF, 128), jnp.bfloat16),
        pltpu.VMEM((HALF, 128), jnp.bfloat16),
        pltpu.VMEM((6, 256, 128), jnp.bfloat16),
        pltpu.VMEM((2, 256, 128), jnp.bfloat16),
        pltpu.VMEM((6, 64, 128), jnp.bfloat16),
        pltpu.VMEM((128, 128), jnp.bfloat16),
        pltpu.VMEM((7, 16, 128), jnp.bfloat16),
        pltpu.SemaphoreType.DMA((40,)),
        pltpu.SemaphoreType.DMA((40,)),
    )

    def __init__(self, place, group, source, result, scratch):
        self.place = place
        self.source = source
        self.base = group * GROUP_ROWS
        self.result = result
        (self.from_core, self.one, self.in_two, self.two, self.in_three, self.three, self.in_four,
         self.send, self.recv) = scratch

    def copy(self, slot, source, target, peer):
        copy = pltpu.make_async_remote_copy(
            src_ref=source,
            dst_ref=target,
            send_sem=self.send.at[slot],
            recv_sem=self.recv.at[slot],
            device_id=peer,
            device_id_type=MESH,
        )
        copy.start()
        return copy

    def core_out(self):
        other = rows((1 - self.place.core) * HALF, HALF)
        self.core_copy = self.copy(0, self.source.at[other], self.from_core, self.place.other_core())

    def core_in(self):
        p = self.place
        self.core_copy.wait()
        own = self.source[rows(p.core * HALF, HALF)]
        self.one[...] = (own.astype(jnp.float32) + self.from_core[...].astype(jnp.float32)).astype(jnp.bfloat16)
        self.copies = []
        for step in range(1, 4):
            x, y = lax.rem(p.x + step, 4), lax.rem(p.y + step, 4)
            self.copies.append(
                self.copy(step, self.one.at[rows(x * 256, 256)], self.in_two.at[step - 1], p.at_x(x)))
            self.copies.append(
                self.copy(3 + step, self.one.at[rows(1024 + y * 256, 256)], self.in_two.at[2 + step], p.at_y(y)))

    def two_in(self):
        p = self.place
        for copy in self.copies:
            copy.wait()
        for part, own in ((0, p.x * 256), (1, 1024 + p.y * 256)):
            total = self.one[rows(own, 256)].astype(jnp.float32)
            for step in range(3):
                total = total + self.in_two[part * 3 + step].astype(jnp.float32)
            self.two[part] = total.astype(jnp.bfloat16)
        self.copies = []
        for step in range(1, 4):
            x, y = lax.rem(p.x + step, 4), lax.rem(p.y + step, 4)
            self.copies.append(
                self.copy(6 + step, self.two.at[0, rows(y * 64, 64)], self.in_three.at[step - 1], p.at_y(y)))
            self.copies.append(
                self.copy(9 + step, self.two.at[1, rows(x * 64, 64)], self.in_three.at[2 + step], p.at_x(x)))

    def three_in(self):
        p = self.place
        for copy in self.copies:
            copy.wait()
        for part, own in ((0, p.y * 64), (1, p.x * 64)):
            total = self.two[part, rows(own, 64)].astype(jnp.float32)
            for step in range(3):
                total = total + self.in_three[part * 3 + step].astype(jnp.float32)
            self.three[part * 64 : part * 64 + 64] = total.astype(jnp.bfloat16)
        self.copies = []
        for step in range(1, 8):
            z = lax.rem(p.z + step, 8)
            self.copies.append(
                self.copy(12 + step, self.three.at[rows(z * 16, 16)], self.in_four.at[step - 1], p.at_z(z)))

    def four_in(self):
        p = self.place
        for copy in self.copies:
            copy.wait()
        total = self.three[rows(p.z * 16, 16)].astype(jnp.float32)
        for step in range(7):
            total = total + self.in_four[step].astype(jnp.float32)
        half = self.base + p.core * HALF
        self.first = half + p.x * 256 + p.y * 64
        self.second = half + 1024 + p.y * 256 + p.x * 64
        upper = lax.div(p.z, 4)
        own = (1 - upper) * self.first + upper * self.second + lax.rem(p.z, 4) * 16
        self.result[rows(own, 16)] = total.astype(jnp.bfloat16)
        self.copies = []
        for step in range(1, 8):
            z = lax.rem(p.z + step, 8)
            tile = self.result.at[rows(own, 16)]
            self.copies.append(self.copy(19 + step, tile, tile, p.at_z(z)))

    def z_gathered(self):
        p = self.place
        for copy in self.copies:
            copy.wait()
        first, second = self.result.at[rows(self.first, 64)], self.result.at[rows(self.second, 64)]
        self.copies = []
        for step in range(1, 4):
            x, y = lax.rem(p.x + step, 4), lax.rem(p.y + step, 4)
            self.copies.append(self.copy(26 + step, first, first, p.at_y(y)))
            self.copies.append(self.copy(29 + step, second, second, p.at_x(x)))

    def one_gathered(self):
        p = self.place
        for copy in self.copies:
            copy.wait()
        half = self.base + p.core * HALF
        first = self.result.at[rows(half + p.x * 256, 256)]
        second = self.result.at[rows(half + 1024 + p.y * 256, 256)]
        self.copies = []
        for step in range(1, 4):
            x, y = lax.rem(p.x + step, 4), lax.rem(p.y + step, 4)
            self.copies.append(self.copy(32 + step, first, first, p.at_x(x)))
            self.copies.append(self.copy(35 + step, second, second, p.at_y(y)))

    def both_gathered(self):
        p = self.place
        for copy in self.copies:
            copy.wait()
        own = self.result.at[rows(self.base + p.core * HALF, HALF)]
        self.core_copy = self.copy(39, own, own, p.other_core())

    def finish(self):
        self.core_copy.wait()


class SmallSum:
    SCRATCH = (
        pltpu.VMEM((2, SMALL_ROWS, 256), jnp.float32),
        pltpu.VMEM((4, SMALL_ROWS, 256), jnp.float32),
        pltpu.VMEM((4, SMALL_ROWS, 256), jnp.float32),
        pltpu.VMEM((8, SMALL_ROWS, 256), jnp.float32),
        pltpu.SemaphoreType.DMA((14,)),
        pltpu.SemaphoreType.DMA((14,)),
    )

    def __init__(self, place, scratch):
        self.place = place
        self.slots = scratch[:4]
        self.send, self.recv = scratch[4:]
        self.stage = -1

    def out(self, value):
        p = self.place
        self.stage += 1
        slots = self.slots[self.stage]
        mine = (p.core, p.x, p.y, p.z)[self.stage]
        at = (lambda _: p.other_core(), p.at_x, p.at_y, p.at_z)[self.stage]
        first = (0, 1, 4, 7)[self.stage]
        count = slots.shape[0]
        slots[mine] = value
        self.copies = []
        for step in range(1, count):
            copy = pltpu.make_async_remote_copy(
                src_ref=slots.at[mine],
                dst_ref=slots.at[mine],
                send_sem=self.send.at[first + step - 1],
                recv_sem=self.recv.at[first + step - 1],
                device_id=at(lax.rem(mine + step, count)),
                device_id_type=MESH,
            )
            copy.start()
            self.copies.append(copy)

    def total(self):
        for copy in self.copies:
            copy.wait()
        slots = self.slots[self.stage]
        total = slots[0]
        for index in range(1, slots.shape[0]):
            total = total + slots[index]
        return total


def dot(left, right):
    return lax.dot_general(left, right, (((1,), (0,)), ((), ())), preferred_element_type=jnp.float32)


def dot_back(grad, weight):
    return lax.dot_general(grad, weight, (((1,), (1,)), ((), ())), preferred_element_type=jnp.float32)


def dot_weight(inputs, grad):
    return lax.dot_general(inputs, grad, (((0,), (0,)), ((), ())), preferred_element_type=jnp.float32)


def low(value):
    return value.astype(jnp.bfloat16)


def wide(value):
    return value.astype(jnp.float32)


def halves(value):
    upper = low(value)
    return upper, low(value - wide(upper))


def ones(mask):
    return low(jnp.where(mask, 1.0, 0.0))


def iota(shape, axis):
    return lax.broadcasted_iota(jnp.int32, shape, axis)


def norm(stream, gain):
    inverse = lax.rsqrt(jnp.mean(stream * stream, axis=-1, keepdims=True) + EPS)
    unit = stream * inverse
    return unit, inverse, low(unit * gain)


def norm_back(grad, unit, inverse, gain):
    scaled = grad * gain
    along = jnp.mean(scaled * unit, axis=-1, keepdims=True)
    return inverse * (scaled - unit * along), jnp.sum(grad * unit, axis=0, keepdims=True)


def over_neighbours(value):
    value = value + pltpu.roll(value, 64, 1)
    value = value + pltpu.roll(value, 32, 1)
    return value + pltpu.roll(value, 16, 1)


class Attention:
    def __init__(self, gather_ref, spread_ref, count, key, value, allowed):
        self.gather_ref = gather_ref
        self.spread_ref = spread_ref
        self.count = count
        self.key = key
        self.value = value
        self.allowed = allowed

    def gather(self, products):
        total = jnp.zeros((TOKENS, 128), jnp.float32)
        for index in range(self.count):
            matrix = self.gather_ref[index * WIDTH : (index + 1) * WIDTH]
            upper, lower = halves(products(index))
            total = total + dot(upper, matrix) + dot(lower, matrix)
        return total

    def spread(self, small, index):
        both = jnp.concatenate(halves(small), axis=1)
        return dot(both, self.spread_ref[:, index * WIDTH : (index + 1) * WIDTH])

    def forward(self, query):
        score = self.gather(lambda index: query * self.key(index))
        self.capped = jnp.tanh(score * (1.0 / (ROOT * CAP)))
        weight = jnp.where(self.allowed, jnp.exp(CAP * self.capped), 0.0)
        self.share = weight / over_neighbours(weight)
        mixed = jnp.zeros((TOKENS, WIDTH), jnp.float32)
        for index in range(self.count):
            mixed = mixed + self.spread(self.share, index) * self.value(index)
        return mixed

    def backward(self, query, grad, put):
        grad_share = self.gather(lambda index: grad * self.value(index))
        along = over_neighbours(self.share * grad_share)
        grad_score = self.share * (grad_share - along) * (1.0 - self.capped * self.capped) * (1.0 / ROOT)
        grad_query = jnp.zeros((TOKENS, WIDTH), jnp.float32)
        for index in range(self.count):
            spread = self.spread(grad_score, index)
            grad_query = grad_query + spread * self.key(index)
            put(index, spread * query, self.spread(self.share, index) * grad)
        return grad_query


def turn(value, by):
    return pltpu.roll(value.reshape(TOKENS // 8, 8, -1), by, 1).reshape(TOKENS, -1)


def window_kernel(
    tokens_ref,
    syndrome_ref,
    step_ref,
    offsets_ref,
    flip_ref,
    embedding_ref,
    gain_tanner_ref,
    w_query_ref,
    w_key_value_ref,
    w_merge_ref,
    gain_time_ref,
    w_temporal_ref,
    w_temporal_out_ref,
    gain_ffn_ref,
    w_up_ref,
    w_down_ref,
    cotangent_ref,
    result_ref,
    small_result_ref,
    token_grad_ref,
    early_ref,
    late_ref,
    gather_ref,
    spread_ref,
    hidden_ref,
    back_out_ref,
    back_in_ref,
    ahead_ref,
    near_ref,
    padded_ref,
    grad_key_value_ref,
    activated_ref,
    before_ref,
    packed_ref,
    grad_packed_ref,
    halo_send,
    halo_recv,
    *scratch,
):
    place = Place()
    barrier, greeted = greet(place.greeted())
    per = len(Sum.SCRATCH)
    early = Sum(place, 0, early_ref, result_ref, scratch[:per])
    late = Sum(place, 1, late_ref, result_ref, scratch[per : 2 * per])
    small = SmallSum(place, scratch[2 * per :])

    def send(slot, source, target, peer):
        copy = pltpu.make_async_remote_copy(
            src_ref=source,
            dst_ref=target,
            send_sem=halo_send.at[slot],
            recv_sem=halo_recv.at[slot],
            device_id=peer,
            device_id_type=MESH,
        )
        copy.start()
        return copy

    code = low(wide(step_ref[...] + 16 * syndrome_ref[...]))
    site_row = ones(lax.div(iota((TOKENS, 32), 0), 8) == iota((TOKENS, 32), 1))
    site_column = lax.rem(iota((TOKENS, 8), 0), 8) == iota((TOKENS, 8), 1)
    code = jnp.sum(jnp.where(site_column, dot(site_row, code), 0.0), axis=1, keepdims=True)
    lane = iota((TOKENS, 16), 1)
    lane_value = wide(lane)
    flipped = jnp.where(code > 15.5, 1.0, 0.0)
    on_step = jnp.where(code - 16.0 * flipped == lane_value, 1.0, 0.0)
    features = low(jnp.where(lane < 8, on_step, jnp.where(lane == 8, flipped, 0.0)))
    table = jnp.concatenate(
        [embedding_ref[...], jnp.broadcast_to(flip_ref[...], (8, WIDTH))], axis=0)
    upper = low(table)
    middle, lower = halves(table - wide(upper))
    embedded = wide(tokens_ref[...]) + (dot(features, upper) + (dot(features, middle) + dot(features, lower)))
    unit_one, inverse_one, hidden_one = norm(embedded, gain_tanner_ref[...])
    hidden_ref[:TOKENS] = hidden_one
    pl.semaphore_wait(barrier, greeted)
    own_hidden = hidden_ref.at[pl.ds(0, TOKENS)]
    ahead_rows = send(0, own_hidden, hidden_ref.at[pl.ds(TOKENS, TOKENS)], place.row_tile(15))
    ahead_columns = send(1, own_hidden, hidden_ref.at[pl.ds(2 * TOKENS, TOKENS)], place.column_tile(15))

    shape = (NEIGHBOURS * WIDTH, 128)
    feature = iota(shape, 0)
    gather_ref[...] = ones(
        lax.div(feature, WIDTH) * 16 + lax.div(lax.rem(feature, WIDTH), HEADDIM) == iota(shape, 1))
    shape = (256, NEIGHBOURS * WIDTH)
    feature = iota(shape, 1)
    spread_ref[...] = ones(
        lax.div(feature, WIDTH) * 16 + lax.div(lax.rem(feature, WIDTH), HEADDIM) == lax.rem(iota(shape, 0), 128))

    query = wide(low(dot(hidden_one, w_query_ref[...])))
    own = wide(low(dot(hidden_one, w_key_value_ref[...])))
    near_ref[0] = own
    ahead_ref[:, 0:8] = own.reshape(ROUNDS, 8, 8, 2 * WIDTH)
    ahead_rows.wait()
    rows_ahead = wide(low(dot(hidden_ref[TOKENS : 2 * TOKENS], w_key_value_ref[...])))
    near_ref[1] = rows_ahead
    ahead_ref[:, 8:16] = rows_ahead.reshape(ROUNDS, 8, 8, 2 * WIDTH)
    for index in (5, 6):
        near_ref[index] = ahead_ref[:, pl.ds(offsets_ref[index - 1, 0], 8)].reshape(TOKENS, 2 * WIDTH)
    ahead_columns.wait()
    columns_ahead = wide(low(dot(hidden_ref[2 * TOKENS :], w_key_value_ref[...])))
    near_ref[4] = columns_ahead
    column = lax.rem(iota((TOKENS, 1), 0), 8)
    for index in (2, 3):
        by = offsets_ref[index - 1, 1]
        near_ref[index] = jnp.where(column < 8 - by, turn(own, 8 - by), turn(columns_ahead, 8 - by))
    lanes = iota((TOKENS, 128), 1)
    tanner = Attention(
        gather_ref,
        spread_ref,
        NEIGHBOURS,
        lambda index: near_ref[index, :, :WIDTH],
        lambda index: near_ref[index, :, WIDTH:],
        lanes < NEIGHBOURS * 16,
    )
    mixed_one = low(tanner.forward(query))
    after_tanner = embedded + dot(mixed_one, w_merge_ref[...])

    unit_two, inverse_two, hidden_two = norm(after_tanner, gain_time_ref[...])
    packed_ref[...] = wide(low(dot(hidden_two, w_temporal_ref[...])))
    time_query = packed_ref[:, :WIDTH]

    def of_round(index, column):
        value = packed_ref[index * 64 : index * 64 + 64, column : column + WIDTH]
        return jnp.concatenate([value] * ROUNDS, axis=0)

    temporal = Attention(
        gather_ref,
        spread_ref,
        ROUNDS,
        lambda index: of_round(index, WIDTH),
        lambda index: of_round(index, 2 * WIDTH),
        lax.div(lanes, 16) <= lax.div(iota((TOKENS, 128), 0), 64),
    )
    mixed_two = low(temporal.forward(time_query))
    after_time = after_tanner + dot(mixed_two, w_temporal_out_ref[...])

    def put(target, slab, value):
        for half in range(value.shape[1] // 128):
            target[(slab + half) * 256 : (slab + half + 1) * 256] = low(value[:, half * 128 : half * 128 + 128])

    unit_three, inverse_three, hidden_three = norm(after_time, gain_ffn_ref[...])
    cotangent = cotangent_ref[...]
    for block in range(FF // WIDTH):
        part = slice(block * WIDTH, (block + 1) * WIDTH)
        before = dot(hidden_three, w_up_ref[:, part])
        square = before * before
        bend = jnp.tanh(GELU * before * (1.0 + 0.044715 * square))
        activated_ref[:, part] = low(0.5 * before * (1.0 + bend))
        slope = 0.5 * (1.0 + bend) + 0.5 * before * (1.0 - bend * bend) * (GELU * (1.0 + 3 * 0.044715 * square))
        before_ref[:, part] = low(dot_back(cotangent, w_down_ref[part]) * slope)
    for block in range(FF // WIDTH):
        part = slice(block * WIDTH, (block + 1) * WIDTH)
        put(early_ref, 2 * block, dot_weight(activated_ref[:, part], cotangent))
    put(early_ref, 8, dot_weight(hidden_three, before_ref[...]))
    early.core_out()
    grad_three = dot_back(before_ref[...], w_up_ref[...])
    grad_norm, grad_gain_ffn = norm_back(grad_three, unit_three, inverse_three, gain_ffn_ref[...])
    grad_after_time = wide(cotangent) + grad_norm

    grad_low = low(grad_after_time)
    put(late_ref, 14, dot_weight(mixed_two, grad_low))
    grad_mixed = dot_back(grad_low, w_temporal_out_ref[...])
    early.core_in()

    def over_rounds(value):
        return (value[:64] + value[64:128]) + (value[128:192] + value[192:])

    def put_time(index, grad_key, grad_value):
        grad_packed_ref[index * 64 : index * 64 + 64, WIDTH : 2 * WIDTH] = low(over_rounds(grad_key))
        grad_packed_ref[index * 64 : index * 64 + 64, 2 * WIDTH :] = low(over_rounds(grad_value))

    grad_packed_ref[:, :WIDTH] = low(temporal.backward(time_query, grad_mixed, put_time))
    put(late_ref, 8, dot_weight(hidden_two, grad_packed_ref[...]))
    grad_two = dot_back(grad_packed_ref[...], w_temporal_ref[...])
    grad_norm, grad_gain_time = norm_back(grad_two, unit_two, inverse_two, gain_time_ref[...])
    grad_after_tanner = grad_after_time + grad_norm
    early.two_in()

    grad_low = low(grad_after_tanner)
    put(late_ref, 6, dot_weight(mixed_one, grad_low))
    grad_mixed = dot_back(grad_low, w_merge_ref[...])
    for index in range(2):
        padded_ref[index, :, 0:8] = jnp.zeros((ROUNDS, 8, 8, 2 * WIDTH), jnp.float32)
        padded_ref[index, :, 16:24] = jnp.zeros((ROUNDS, 8, 8, 2 * WIDTH), jnp.float32)

    def put_tanner(index, grad_key, grad_value):
        grad = jnp.concatenate([grad_key, grad_value], axis=1)
        if index == 0:
            grad_key_value_ref[0] = grad
        elif index == 1:
            grad_key_value_ref[1] = grad
        elif index == 4:
            grad_key_value_ref[2] = grad
        elif index in (2, 3):
            by = offsets_ref[index - 1, 1]
            turned = turn(grad, by)
            near_ref[index] = jnp.where(column >= by, turned, 0.0)
            near_ref[index + 2] = jnp.where(column >= by, 0.0, turned)
        else:
            padded_ref[index - 5, :, 8:16] = grad.reshape(ROUNDS, 8, 8, 2 * WIDTH)

    kept = {}

    def hold(index, grad_key, grad_value):
        kept[index] = (grad_key, grad_value)

    grad_query = tanner.backward(query, grad_mixed, hold)
    for index in (0, 1, 4, 5, 6, 2, 3):
        put_tanner(index, *kept[index])
    own_grad = grad_key_value_ref[0] + near_ref[2] + near_ref[3]
    rows_grad = grad_key_value_ref[1]
    for index in (5, 6):
        by = offsets_ref[index - 1, 0]
        own_grad = own_grad + padded_ref[index - 5, :, pl.ds(8 - by, 8)].reshape(TOKENS, 2 * WIDTH)
        rows_grad = rows_grad + padded_ref[index - 5, :, pl.ds(16 - by, 8)].reshape(TOKENS, 2 * WIDTH)
    columns_grad = grad_key_value_ref[2] + near_ref[4] + near_ref[5]
    rows_low, columns_low, own_low = low(rows_grad), low(columns_grad), low(own_grad)
    back_out_ref[0] = low(dot_back(rows_low, w_key_value_ref[...]))
    back_rows = send(2, back_out_ref.at[0], back_in_ref.at[0], place.row_tile(1))
    back_out_ref[1] = low(dot_back(columns_low, w_key_value_ref[...]))
    back_columns = send(3, back_out_ref.at[1], back_in_ref.at[1], place.column_tile(1))
    early.three_in()
    query_low = low(grad_query)
    put(late_ref, 0, dot_weight(hidden_one, query_low))
    put(
        late_ref,
        2,
        dot_weight(hidden_one, own_low)
        + dot_weight(hidden_ref[TOKENS : 2 * TOKENS], rows_low)
        + dot_weight(hidden_ref[2 * TOKENS :], columns_low),
    )
    late.core_out()
    early.four_in()
    grad_one = dot_back(query_low, w_query_ref[...]) + dot_back(own_low, w_key_value_ref[...])
    late.core_in()
    back_rows.wait()
    back_columns.wait()
    grad_one = grad_one + (wide(back_in_ref[0]) + wide(back_in_ref[1]))
    grad_norm, grad_gain_tanner = norm_back(grad_one, unit_one, inverse_one, gain_tanner_ref[...])
    grad_embedded = grad_after_tanner + grad_norm
    token_grad_ref[...] = low(grad_embedded)
    upper, lower = halves(grad_embedded)
    from_table = dot_weight(features, upper) + dot_weight(features, lower)
    row = iota((SMALL_ROWS, WIDTH), 0)
    shares = jnp.where(row == 9, grad_gain_tanner, from_table)
    shares = jnp.where(row == 10, grad_gain_time, shares)
    shares = jnp.where(row == 11, grad_gain_ffn, shares)
    small.out(shares)
    early.z_gathered()
    late.two_in()
    small.out(small.total())
    early.one_gathered()
    late.three_in()
    small.out(small.total())
    early.both_gathered()
    late.four_in()
    small.out(small.total())
    late.z_gathered()
    small_result_ref[...] = small.total()
    late.one_gathered()
    late.both_gathered()
    early.finish()
    late.finish()


def window(*operands):
    vmem = pl.BlockSpec(memory_space=pltpu.VMEM)
    specs = [vmem] * len(operands)
    specs[3] = pl.BlockSpec(memory_space=pltpu.SMEM)
    bf16, f32 = jnp.bfloat16, jnp.float32
    return pl.pallas_call(
        window_kernel,
        name="window",
        out_shape=(
            jax.ShapeDtypeStruct((2 * GROUP_ROWS, 128), bf16),
            jax.ShapeDtypeStruct((SMALL_ROWS, WIDTH), f32),
            jax.ShapeDtypeStruct((TOKENS, WIDTH), bf16),
        ),
        in_specs=specs,
        out_specs=(vmem, vmem, vmem),
        scratch_shapes=[
            pltpu.VMEM((GROUP_ROWS, 128), bf16),
            pltpu.VMEM((GROUP_ROWS, 128), bf16),
            pltpu.VMEM((NEIGHBOURS * WIDTH, 128), bf16),
            pltpu.VMEM((256, NEIGHBOURS * WIDTH), bf16),
            pltpu.VMEM((3 * TOKENS, WIDTH), bf16),
            pltpu.VMEM((2, TOKENS, WIDTH), bf16),
            pltpu.VMEM((2, TOKENS, WIDTH), bf16),
            pltpu.VMEM((ROUNDS, 16, 8, 2 * WIDTH), f32),
            pltpu.VMEM((NEIGHBOURS, TOKENS, 2 * WIDTH), f32),
            pltpu.VMEM((2, ROUNDS, 24, 8, 2 * WIDTH), f32),
            pltpu.VMEM((3, TOKENS, 2 * WIDTH), f32),
            pltpu.VMEM((TOKENS, FF), bf16),
            pltpu.VMEM((TOKENS, FF), bf16),
            pltpu.VMEM((TOKENS, 3 * WIDTH), f32),
            pltpu.VMEM((TOKENS, 3 * WIDTH), bf16),
            pltpu.SemaphoreType.DMA((4,)),
            pltpu.SemaphoreType.DMA((4,)),
            *Sum.SCRATCH,
            *Sum.SCRATCH,
            *SmallSum.SCRATCH,
        ],
        compiler_params=pltpu.CompilerParams(
            collective_id=0, has_side_effects=True, vmem_limit_bytes=56 * 2**20),
    )(*operands)


def finish_kernel(scale, slabs_ref, small_ref, token_grad_in_ref, *outs):
    (token_grad_ref, flip_ref, plan_ref, gain_tanner_ref, query_ref, key_value_ref, merge_ref,
     gain_time_ref, temporal_ref, temporal_out_ref, gain_ffn_ref, up_ref, down_ref) = outs
    token_grad_ref[...] = token_grad_in_ref[...]
    small = small_ref[...] * scale
    plan_ref[...] = small[:8]
    flip_ref[...] = small[8:9]
    gain_tanner_ref[...] = small[9:10]
    gain_time_ref[...] = small[10:11]
    gain_ffn_ref[...] = small[11:12]

    def take(target, slab):
        for block in range(target.shape[0] // 256):
            for half in range(target.shape[1] // 128):
                target[block * 256 : block * 256 + 256, half * 128 : half * 128 + 128] = (
                    wide(slabs_ref[slab * 256 : slab * 256 + 256]) * scale)
                slab += 1

    take(down_ref, 0)
    take(up_ref, 8)
    take(query_ref, 16)
    take(key_value_ref, 18)
    take(merge_ref, 22)
    take(temporal_ref, 24)
    take(temporal_out_ref, 30)


def finish(scale, slabs, small, token_grad):
    vmem = pl.BlockSpec(memory_space=pltpu.VMEM)
    f32 = jnp.float32
    return pl.pallas_call(
        lambda *refs: finish_kernel(scale, *refs),
        name="finish",
        out_shape=(
            jax.ShapeDtypeStruct((TOKENS, WIDTH), jnp.bfloat16),
            jax.ShapeDtypeStruct((1, WIDTH), f32),
            jax.ShapeDtypeStruct((PLAN_STEP_COUNT, WIDTH), f32),
            jax.ShapeDtypeStruct((1, WIDTH), f32),
            jax.ShapeDtypeStruct((WIDTH, WIDTH), f32),
            jax.ShapeDtypeStruct((WIDTH, 2 * WIDTH), f32),
            jax.ShapeDtypeStruct((WIDTH, WIDTH), f32),
            jax.ShapeDtypeStruct((1, WIDTH), f32),
            jax.ShapeDtypeStruct((WIDTH, 3 * WIDTH), f32),
            jax.ShapeDtypeStruct((WIDTH, WIDTH), f32),
            jax.ShapeDtypeStruct((1, WIDTH), f32),
            jax.ShapeDtypeStruct((WIDTH, FF), f32),
            jax.ShapeDtypeStruct((FF, WIDTH), f32),
        ),
        in_specs=[vmem] * 3,
        out_specs=(vmem,) * 13,
        compiler_params=pltpu.CompilerParams(vmem_limit_bytes=32 * 2**20),
    )(slabs, small, token_grad)


def on_device(
    tokens,
    syndrome,
    check_plan_step,
    offsets,
    flip_vector,
    plan_step_embedding,
    gain_tanner,
    w_query,
    w_key_value,
    w_merge,
    gain_time,
    w_temporal,
    w_temporal_out,
    gain_ffn,
    w_ffn_up,
    w_ffn_down,
    cotangent,
):
    tile = tokens.shape
    devices = lax.axis_size("gx") * lax.axis_size("gy")
    scale = 1.0 / math.sqrt(tile[0] * tile[1] * tile[2] * devices)
    slabs, small, token_grad = window(
        tokens.reshape(TOKENS, WIDTH),
        syndrome.reshape(TOKENS // 8, 8),
        check_plan_step.reshape(TOKENS // 8, 8),
        offsets,
        flip_vector.reshape(1, WIDTH),
        plan_step_embedding,
        gain_tanner.reshape(1, WIDTH),
        w_query,
        w_key_value,
        w_merge,
        gain_time.reshape(1, WIDTH),
        w_temporal,
        w_temporal_out,
        gain_ffn.reshape(1, WIDTH),
        w_ffn_up,
        w_ffn_down,
        cotangent.reshape(TOKENS, WIDTH),
    )
    outs = list(finish(scale, slabs, small, token_grad))
    outs[0] = outs[0].reshape(tile)
    for index in (1, 3, 7, 10):
        outs[index] = outs[index].reshape(WIDTH)
    return tuple(outs)


def solution(mesh):
    return jax.shard_map(
        on_device,
        mesh=mesh,
        in_specs=(
            P(None, "gx", "gy", None),
            P(None, "gx", "gy"),
            P(None, "gx", "gy"),
            P(),
            P(),
            P(),
            P(),
            P(),
            P(),
            P(),
            P(),
            P(),
            P(),
            P(),
            P(),
            P(),
            P(None, "gx", "gy", None),
        ),
        out_specs=(
            P(None, "gx", "gy", None),
            P(),
            P(),
            P(),
            P(),
            P(),
            P(),
            P(),
            P(),
            P(),
            P(),
            P(),
            P(),
        ),
        check_vma=False,
    )
```

```python
import math

import jax
import jax.numpy as jnp
from jax import lax
from jax.experimental import pallas as pl
from jax.experimental.pallas import tpu as pltpu
from jax.sharding import PartitionSpec as P

WIDTH = 256
HEADDIM = 32
FF = 1024
PLAN_STEP_COUNT = 8
TOKENS = 256
NEIGHBOURS = 7
ROUNDS = 4
EPS = 1e-05
CAP = 4.0
ROOT = math.sqrt(HEADDIM)
GELU = math.sqrt(2 / math.pi)

MESH = pl.DeviceIdType.MESH
HALF = 1024
RESULT_ROWS = 8 * HALF
PLANE_STEPS = sorted(
    [(x, y) for x in range(4) for y in range(4) if x or y], key=lambda at: -(at[0] % 2 + at[1] % 2 + 2 * (at[0] == 2) + 2 * (at[1] == 2)))
Z_STEPS = (4, 3, 5, 2, 6, 1, 7)
SMALL_ROWS = 16


class Place:
    def __init__(self):
        self.gx = lax.axis_index("gx")
        self.gy = lax.axis_index("gy")
        self.z = lax.rem(self.gx, 8)
        self.y_lo = lax.div(self.gx, 8)
        self.core = lax.rem(self.gy, 2)
        self.y_hi = lax.rem(lax.div(self.gy, 2), 2)
        self.x = lax.div(self.gy, 4)
        self.y = self.y_hi * 2 + self.y_lo

    def other_core(self):
        return (self.gx, self.gy + 1 - 2 * self.core)

    def at_x(self, x):
        return (self.gx, x * 4 + self.y_hi * 2 + self.core)

    def at_y(self, y):
        return (lax.rem(y, 2) * 8 + self.z, self.x * 4 + lax.div(y, 2) * 2 + self.core)

    def in_plane(self, x, y):
        return (lax.rem(y, 2) * 8 + self.z, x * 4 + lax.div(y, 2) * 2 + self.core)

    def at_z(self, z):
        return (self.y_lo * 8 + z, self.gy)

    def greeted(self):
        peers = [self.row_tile(1), self.column_tile(1), self.row_tile(15), self.column_tile(15)]
        peers.append(self.other_core())
        for step_x, step_y in PLANE_STEPS:
            peers.append(self.in_plane(lax.rem(self.x + step_x, 4), lax.rem(self.y + step_y, 4)))
        for step in range(1, 8):
            peers.append(self.at_z(lax.rem(self.z + step, 8)))
        return peers

    def row_tile(self, step):
        return (lax.rem(self.gx + step, 16), self.gy)

    def column_tile(self, step):
        return (self.gx, lax.rem(self.gy + step, 16))


def greet(peers):
    barrier = pltpu.get_barrier_semaphore()
    for peer in peers:
        pl.semaphore_signal(barrier, inc=1, device_id=peer, device_id_type=MESH)
    return barrier, len(peers)


def rows(start, count):
    return pl.ds(pl.multiple_of(start, min(count, 16)), count)


class Sum:
    @staticmethod
    def scratch(half):
        bf16 = jnp.bfloat16
        return (
            pltpu.VMEM((half, 128), bf16),
            pltpu.VMEM((half, 128), bf16),
            pltpu.VMEM((15, half // 16, 128), bf16),
            pltpu.VMEM((8, half // 16, 128), bf16),
            pltpu.SemaphoreType.DMA((54,)),
            pltpu.SemaphoreType.DMA((54,)),
        )

    def __init__(self, place, half, base, source, result, scratch):
        self.place = place
        self.half = half
        self.chunk = half // 16
        self.base = base + place.core * half
        self.source = source
        self.result = result
        self.from_core, self.one, self.in_two, self.along_z, self.send, self.recv = scratch

    def copy(self, slot, source, target, peer):
        copy = pltpu.make_async_remote_copy(
            src_ref=source,
            dst_ref=target,
            send_sem=self.send.at[slot],
            recv_sem=self.recv.at[slot],
            device_id=peer,
            device_id_type=MESH,
        )
        copy.start()
        return copy

    def to_plane(self, slot, source, target):
        p = self.place
        self.copies = []
        for index, (step_x, step_y) in enumerate(PLANE_STEPS):
            x, y = lax.rem(p.x + step_x, 4), lax.rem(p.y + step_y, 4)
            self.copies.append(
                self.copy(slot + index, source((x * 4 + y) * self.chunk), target(index), p.in_plane(x, y)))

    def in_result(self, x, y):
        return self.result.at[rows(self.base + (x * 4 + y) * self.chunk, self.chunk)]

    def core_out(self):
        other = rows((1 - self.place.core) * self.half, self.half)
        self.core_copy = self.copy(0, self.source.at[other], self.from_core, self.place.other_core())

    def core_in(self):
        self.core_copy.wait()
        own = self.source[rows(self.place.core * self.half, self.half)]
        self.one[...] = (own.astype(jnp.float32) + self.from_core[...].astype(jnp.float32)).astype(jnp.bfloat16)
        self.to_plane(
            1, lambda at: self.one.at[rows(at, self.chunk)], lambda index: self.in_two.at[index])

    def plane_in(self):
        p = self.place
        for copy in self.copies:
            copy.wait()
        total = self.one[rows((p.x * 4 + p.y) * self.chunk, self.chunk)].astype(jnp.float32)
        for index in range(15):
            total = total + self.in_two[index].astype(jnp.float32)
        self.along_z[p.z] = total.astype(jnp.bfloat16)
        own = self.along_z.at[p.z]
        self.copies = []
        for index, step in enumerate(Z_STEPS):
            self.copies.append(self.copy(16 + index, own, own, p.at_z(lax.rem(p.z + step, 8))))

    def z_in(self):
        p = self.place
        for copy in self.copies:
            copy.wait()
        total = self.along_z[0].astype(jnp.float32)
        for index in range(1, 8):
            total = total + self.along_z[index].astype(jnp.float32)
        self.result[rows(self.base + (p.x * 4 + p.y) * self.chunk, self.chunk)] = total.astype(jnp.bfloat16)
        own = self.in_result(p.x, p.y)
        self.to_plane(23, lambda at: own, lambda index: own)
        self.core_copies = [self.copy(38, own, own, p.other_core())]

    def plane_gathered(self):
        p = self.place
        for index in reversed(range(15)):
            self.copies[index].wait()
            step_x, step_y = PLANE_STEPS[index]
            chunk = self.in_result(lax.rem(p.x + 4 - step_x, 4), lax.rem(p.y + 4 - step_y, 4))
            self.core_copies.append(self.copy(39 + index, chunk, chunk, p.other_core()))

    def finish(self):
        for copy in self.core_copies:
            copy.wait()


class TwoStepSum(Sum):
    @staticmethod
    def scratch(half):
        bf16 = jnp.bfloat16
        return (
            pltpu.VMEM((half, 128), bf16),
            pltpu.VMEM((half, 128), bf16),
            pltpu.VMEM((6, half // 8, 128), bf16),
            pltpu.VMEM((2, half // 8, 128), bf16),
            pltpu.VMEM((6, half // 32, 128), bf16),
            pltpu.VMEM((8, half // 16, 128), bf16),
            pltpu.SemaphoreType.DMA((40,)),
            pltpu.SemaphoreType.DMA((40,)),
        )

    def __init__(self, place, half, base, source, result, scratch):
        self.place = place
        self.half = half
        self.strip = half // 8
        self.chunk = half // 32
        self.base = base + place.core * half
        self.source = source
        self.result = result
        (self.from_core, self.one, self.in_one, self.two, self.in_two, self.along_z, self.send, self.recv) = scratch

    def both_ways(self, slot, first_along_x, first, second, first_target, second_target):
        p = self.place
        self.copies = []
        for index, step in enumerate((2, 1, 3)):
            x, y = lax.rem(p.x + step, 4), lax.rem(p.y + step, 4)
            of_first, of_second = ((x, p.at_x(x)), (y, p.at_y(y)))[:: 1 if first_along_x else -1]
            self.copies.append(
                self.copy(slot + index, first(of_first[0]), first_target(index), of_first[1]))
            self.copies.append(
                self.copy(slot + 3 + index, second(of_second[0]), second_target(index), of_second[1]))

    def core_in(self):
        self.core_copy.wait()
        own = self.source[rows(self.place.core * self.half, self.half)]
        self.one[...] = (own.astype(jnp.float32) + self.from_core[...].astype(jnp.float32)).astype(jnp.bfloat16)
        middle = self.half // 2
        self.both_ways(
            1,
            True,
            lambda x: self.one.at[rows(x * self.strip, self.strip)],
            lambda y: self.one.at[rows(middle + y * self.strip, self.strip)],
            lambda index: self.in_one.at[index],
            lambda index: self.in_one.at[3 + index],
        )

    def strip_in(self):
        p = self.place
        for copy in self.copies:
            copy.wait()
        for part, own in ((0, p.x * self.strip), (1, self.half // 2 + p.y * self.strip)):
            total = self.one[rows(own, self.strip)].astype(jnp.float32)
            for index in range(3):
                total = total + self.in_one[part * 3 + index].astype(jnp.float32)
            self.two[part] = total.astype(jnp.bfloat16)
        self.both_ways(
            7,
            False,
            lambda y: self.two.at[0, rows(y * self.chunk, self.chunk)],
            lambda x: self.two.at[1, rows(x * self.chunk, self.chunk)],
            lambda index: self.in_two.at[index],
            lambda index: self.in_two.at[3 + index],
        )

    def plane_in(self):
        p = self.place
        for copy in self.copies:
            copy.wait()
        for part, own in ((0, p.y * self.chunk), (1, p.x * self.chunk)):
            total = self.two[part, rows(own, self.chunk)].astype(jnp.float32)
            for index in range(3):
                total = total + self.in_two[part * 3 + index].astype(jnp.float32)
            self.along_z[p.z, part * self.chunk : (part + 1) * self.chunk] = total.astype(jnp.bfloat16)
        own = self.along_z.at[p.z]
        self.copies = []
        for index, step in enumerate(Z_STEPS):
            self.copies.append(self.copy(13 + index, own, own, p.at_z(lax.rem(p.z + step, 8))))

    def z_in(self):
        p = self.place
        for copy in self.copies:
            copy.wait()
        total = self.along_z[0].astype(jnp.float32)
        for index in range(1, 8):
            total = total + self.along_z[index].astype(jnp.float32)
        total = total.astype(jnp.bfloat16)
        first = rows(self.base + p.x * self.strip + p.y * self.chunk, self.chunk)
        second = rows(self.base + self.half // 2 + p.y * self.strip + p.x * self.chunk, self.chunk)
        self.result[first] = total[: self.chunk]
        self.result[second] = total[self.chunk :]
        first, second = self.result.at[first], self.result.at[second]
        self.both_ways(
            20, False, lambda _: first, lambda _: second, lambda _: first, lambda _: second)

    def strip_of(self, part, index):
        return self.result.at[rows(self.base + part * (self.half // 2) + index * self.strip, self.strip)]

    def strip_gathered(self):
        p = self.place
        for copy in self.copies:
            copy.wait()
        first, second = self.strip_of(0, p.x), self.strip_of(1, p.y)
        self.both_ways(
            26, True, lambda _: first, lambda _: second, lambda _: first, lambda _: second)
        self.core_copies = [
            self.copy(32, first, first, p.other_core()), self.copy(33, second, second, p.other_core())]

    def plane_gathered(self):
        p = self.place
        for index in reversed(range(6)):
            self.copies[index].wait()
            part, step = index % 2, (2, 1, 3)[index // 2]
            strip = self.strip_of(part, lax.rem((p.x, p.y)[part] + 4 - step, 4))
            self.core_copies.append(self.copy(34 + index, strip, strip, p.other_core()))


class SmallSum:
    SCRATCH = (
        pltpu.VMEM((2, SMALL_ROWS, 256), jnp.bfloat16),
        pltpu.VMEM((16, SMALL_ROWS, 256), jnp.bfloat16),
        pltpu.VMEM((8, SMALL_ROWS, 256), jnp.bfloat16),
        pltpu.SemaphoreType.DMA((23,)),
        pltpu.SemaphoreType.DMA((23,)),
    )

    def __init__(self, place, scratch):
        self.place = place
        self.slots = scratch[:3]
        self.send, self.recv = scratch[3:]

    def out(self, stage, value):
        p = self.place
        self.stage = stage
        slots = self.slots[stage]
        mine = (p.core, p.x * 4 + p.y, p.z)[stage]
        if stage == 0:
            peers = [p.other_core()]
        elif stage == 1:
            peers = [p.in_plane(lax.rem(p.x + x, 4), lax.rem(p.y + y, 4)) for x, y in PLANE_STEPS]
        else:
            peers = [p.at_z(lax.rem(p.z + step, 8)) for step in Z_STEPS]
        slots[mine] = value.astype(jnp.bfloat16)
        self.copies = []
        for index, peer in enumerate(peers):
            copy = pltpu.make_async_remote_copy(
                src_ref=slots.at[mine],
                dst_ref=slots.at[mine],
                send_sem=self.send.at[(0, 1, 16)[stage] + index],
                recv_sem=self.recv.at[(0, 1, 16)[stage] + index],
                device_id=peer,
                device_id_type=MESH,
            )
            copy.start()
            self.copies.append(copy)

    def total(self):
        for copy in self.copies:
            copy.wait()
        slots = self.slots[self.stage]
        total = slots[0].astype(jnp.float32)
        for index in range(1, slots.shape[0]):
            total = total + slots[index].astype(jnp.float32)
        return total


def dot(left, right):
    return lax.dot_general(left, right, (((1,), (0,)), ((), ())), preferred_element_type=jnp.float32)


def dot_back(grad, weight):
    return lax.dot_general(grad, weight, (((1,), (1,)), ((), ())), preferred_element_type=jnp.float32)


def dot_weight(inputs, grad):
    return lax.dot_general(inputs, grad, (((0,), (0,)), ((), ())), preferred_element_type=jnp.float32)


def low(value):
    return value.astype(jnp.bfloat16)


def wide(value):
    return value.astype(jnp.float32)


def halves(value):
    upper = low(value)
    return upper, low(value - wide(upper))


def ones(mask):
    return low(jnp.where(mask, 1.0, 0.0))


def iota(shape, axis):
    return lax.broadcasted_iota(jnp.int32, shape, axis)


def norm(stream, gain):
    inverse = lax.rsqrt(jnp.mean(stream * stream, axis=-1, keepdims=True) + EPS)
    unit = stream * inverse
    return unit, inverse, low(unit * gain)


def norm_back(grad, unit, inverse, gain):
    scaled = grad * gain
    along = jnp.mean(scaled * unit, axis=-1, keepdims=True)
    return inverse * (scaled - unit * along), jnp.sum(grad * unit, axis=0, keepdims=True)


def over_neighbours(value):
    value = value + pltpu.roll(value, 64, 1)
    value = value + pltpu.roll(value, 32, 1)
    return value + pltpu.roll(value, 16, 1)


class Attention:
    def __init__(self, gather_ref, spread_ref, order, key, value, allowed):
        self.gather_ref = gather_ref
        self.spread_ref = spread_ref
        self.count = len(order)
        self.order = order
        self.key = key
        self.value = value
        self.allowed = allowed

    def gather(self, products):
        total = jnp.zeros((TOKENS, 128), jnp.float32)
        for index in range(self.count):
            matrix = self.gather_ref[index * WIDTH : (index + 1) * WIDTH]
            upper, lower = halves(products(index))
            total = total + dot(upper, matrix) + dot(lower, matrix)
        return total

    def spread(self, small, index):
        both = jnp.concatenate(halves(small), axis=1)
        return dot(both, self.spread_ref[:, index * WIDTH : (index + 1) * WIDTH])

    def forward(self, query):
        score = self.gather(lambda index: query * self.key(index))
        self.capped = jnp.tanh(score * (1.0 / (ROOT * CAP)))
        weight = jnp.where(self.allowed, jnp.exp(CAP * self.capped), 0.0)
        self.share = weight / over_neighbours(weight)
        mixed = jnp.zeros((TOKENS, WIDTH), jnp.float32)
        for index in range(self.count):
            mixed = mixed + self.spread(self.share, index) * self.value(index)
        return mixed

    def backward(self, query, grad, put):
        grad_share = self.gather(lambda index: grad * self.value(index))
        along = over_neighbours(self.share * grad_share)
        grad_score = self.share * (grad_share - along) * (1.0 - self.capped * self.capped) * (1.0 / ROOT)
        grad_query = jnp.zeros((TOKENS, WIDTH), jnp.float32)
        for index in self.order:
            spread = self.spread(grad_score, index)
            grad_query = grad_query + spread * self.key(index)
            put(index, spread * query, self.spread(self.share, index) * grad)
        return grad_query


def turn(value, by):
    return pltpu.roll(value.reshape(TOKENS // 8, 8, -1), by, 1).reshape(TOKENS, -1)


def window_kernel(
    tokens_ref,
    syndrome_ref,
    step_ref,
    offsets_ref,
    flip_ref,
    embedding_ref,
    gain_tanner_ref,
    w_query_hbm,
    w_key_value_hbm,
    w_merge_hbm,
    gain_time_ref,
    w_temporal_hbm,
    w_temporal_out_hbm,
    gain_ffn_ref,
    w_up_hbm,
    w_down_hbm,
    cotangent_hbm,
    result_ref,
    small_result_ref,
    token_grad_ref,
    w_query_ref,
    w_key_value_ref,
    w_merge_ref,
    w_temporal_ref,
    w_temporal_out_ref,
    w_up_ref,
    w_down_ref,
    cotangent_ref,
    loaded,
    early_ref,
    middle_ref,
    late_ref,
    gather_ref,
    spread_ref,
    hidden_ref,
    back_out_ref,
    back_in_ref,
    ahead_ref,
    near_ref,
    padded_ref,
    own_grad_ref,
    rows_grad_ref,
    columns_grad_ref,
    activated_ref,
    before_ref,
    packed_ref,
    grad_packed_ref,
    halo_send,
    halo_recv,
    *scratch,
):
    place = Place()
    barrier, greeted = greet(place.greeted())
    loads = []
    for index, (source, target) in enumerate((
        (w_query_hbm, w_query_ref),
        (w_key_value_hbm, w_key_value_ref),
        (w_merge_hbm, w_merge_ref),
        (w_temporal_hbm, w_temporal_ref),
        (w_temporal_out_hbm, w_temporal_out_ref),
        (w_up_hbm, w_up_ref),
        (w_down_hbm, w_down_ref),
        (cotangent_hbm, cotangent_ref),
    )):
        load = pltpu.make_async_copy(source, target, loaded.at[index])
        load.start()
        loads.append(load)
    groups = ((TwoStepSum, 2 * HALF, 0, early_ref), (TwoStepSum, HALF, 4 * HALF, middle_ref), (TwoStepSum, HALF, 6 * HALF, late_ref))
    ends = [len(SmallSum.SCRATCH)]
    for kind, half, _, _ in groups:
        ends.append(ends[-1] + len(kind.scratch(half)))
    early, middle, late = (
        kind(place, half, base, source, result_ref, scratch[ends[index] : ends[index + 1]])
        for index, (kind, half, base, source) in enumerate(groups))
    small = SmallSum(place, scratch[: ends[0]])

    def send(slot, source, target, peer):
        copy = pltpu.make_async_remote_copy(
            src_ref=source,
            dst_ref=target,
            send_sem=halo_send.at[slot],
            recv_sem=halo_recv.at[slot],
            device_id=peer,
            device_id_type=MESH,
        )
        copy.start()
        return copy

    code = low(wide(step_ref[...] + 16 * syndrome_ref[...]))
    site_row = ones(lax.div(iota((TOKENS, 32), 0), 8) == iota((TOKENS, 32), 1))
    site_column = lax.rem(iota((TOKENS, 8), 0), 8) == iota((TOKENS, 8), 1)
    code = jnp.sum(jnp.where(site_column, dot(site_row, code), 0.0), axis=1, keepdims=True)
    lane = iota((TOKENS, 16), 1)
    lane_value = wide(lane)
    flipped = jnp.where(code > 15.5, 1.0, 0.0)
    on_step = jnp.where(code - 16.0 * flipped == lane_value, 1.0, 0.0)
    features = low(jnp.where(lane < 8, on_step, jnp.where(lane == 8, flipped, 0.0)))
    table = jnp.concatenate(
        [embedding_ref[...], jnp.broadcast_to(flip_ref[...], (8, WIDTH))], axis=0)
    upper = low(table)
    next_upper, lower = halves(table - wide(upper))
    embedded = wide(tokens_ref[...]) + (dot(features, upper) + (dot(features, next_upper) + dot(features, lower)))
    unit_one, inverse_one, hidden_one = norm(embedded, gain_tanner_ref[...])
    hidden_ref[:TOKENS] = hidden_one
    pl.semaphore_wait(barrier, greeted)
    own_hidden = hidden_ref.at[pl.ds(0, TOKENS)]
    ahead_rows = send(0, own_hidden, hidden_ref.at[pl.ds(TOKENS, TOKENS)], place.row_tile(15))
    ahead_columns = send(1, own_hidden, hidden_ref.at[pl.ds(2 * TOKENS, TOKENS)], place.column_tile(15))

    for index in range(2):
        padded_ref[index, :, 0:8] = jnp.zeros((ROUNDS, 8, 8, 2 * WIDTH), jnp.float32)
        padded_ref[index, :, 16:24] = jnp.zeros((ROUNDS, 8, 8, 2 * WIDTH), jnp.float32)

    shape = (NEIGHBOURS * WIDTH, 128)
    feature = iota(shape, 0)
    gather_ref[...] = ones(
        lax.div(feature, WIDTH) * 16 + lax.div(lax.rem(feature, WIDTH), HEADDIM) == iota(shape, 1))
    shape = (256, NEIGHBOURS * WIDTH)
    feature = iota(shape, 1)
    spread_ref[...] = ones(
        lax.div(feature, WIDTH) * 16 + lax.div(lax.rem(feature, WIDTH), HEADDIM) == lax.rem(iota(shape, 0), 128))

    for load in loads[:3]:
        load.wait()
    query = wide(low(dot(hidden_one, w_query_ref[...])))
    own = wide(low(dot(hidden_one, w_key_value_ref[...])))
    near_ref[0] = own
    ahead_ref[:, 0:8] = own.reshape(ROUNDS, 8, 8, 2 * WIDTH)
    ahead_rows.wait()
    rows_ahead = wide(low(dot(hidden_ref[TOKENS : 2 * TOKENS], w_key_value_ref[...])))
    near_ref[1] = rows_ahead
    ahead_ref[:, 8:16] = rows_ahead.reshape(ROUNDS, 8, 8, 2 * WIDTH)
    for index in (5, 6):
        near_ref[index] = ahead_ref[:, pl.ds(offsets_ref[0, index - 1], 8)].reshape(TOKENS, 2 * WIDTH)
    ahead_columns.wait()
    columns_ahead = wide(low(dot(hidden_ref[2 * TOKENS :], w_key_value_ref[...])))
    near_ref[4] = columns_ahead
    column = lax.rem(iota((TOKENS, 1), 0), 8)
    for index in (2, 3):
        by = offsets_ref[1, index - 1]
        near_ref[index] = jnp.where(column < 8 - by, turn(own, 8 - by), turn(columns_ahead, 8 - by))
    lanes = iota((TOKENS, 128), 1)
    tanner = Attention(
        gather_ref,
        spread_ref,
        (0, 1, 4, 2, 3, 5, 6),
        lambda index: near_ref[index, :, :WIDTH],
        lambda index: near_ref[index, :, WIDTH:],
        lanes < NEIGHBOURS * 16,
    )
    mixed_one = low(tanner.forward(query))
    after_tanner = embedded + dot(mixed_one, w_merge_ref[...])

    for load in loads[3:]:
        load.wait()
    unit_two, inverse_two, hidden_two = norm(after_tanner, gain_time_ref[...])
    packed_ref[...] = wide(low(dot(hidden_two, w_temporal_ref[...])))
    time_query = packed_ref[:, :WIDTH]

    def of_round(index, column):
        value = packed_ref[index * 64 : index * 64 + 64, column : column + WIDTH]
        return jnp.concatenate([value] * ROUNDS, axis=0)

    temporal = Attention(
        gather_ref,
        spread_ref,
        (0, 1, 2, 3),
        lambda index: of_round(index, WIDTH),
        lambda index: of_round(index, 2 * WIDTH),
        lax.div(lanes, 16) <= lax.div(iota((TOKENS, 128), 0), 64),
    )
    mixed_two = low(temporal.forward(time_query))
    after_time = after_tanner + dot(mixed_two, w_temporal_out_ref[...])

    def put(target, slab, value):
        for half in range(value.shape[1] // 128):
            target[(slab + half) * 256 : (slab + half + 1) * 256] = low(value[:, half * 128 : half * 128 + 128])

    unit_three, inverse_three, hidden_three = norm(after_time, gain_ffn_ref[...])
    cotangent = cotangent_ref[...]
    for block in range(FF // WIDTH):
        part = slice(block * WIDTH, (block + 1) * WIDTH)
        before = dot(hidden_three, w_up_ref[:, part])
        square = before * before
        bend = jnp.tanh(GELU * before * (1.0 + 0.044715 * square))
        activated_ref[:, part] = low(0.5 * before * (1.0 + bend))
        slope = 0.5 * (1.0 + bend) + 0.5 * before * (1.0 - bend * bend) * (GELU * (1.0 + 3 * 0.044715 * square))
        before_ref[:, part] = low(dot_back(cotangent, w_down_ref[part]) * slope)
    for block in range(FF // WIDTH):
        part = slice(block * WIDTH, (block + 1) * WIDTH)
        put(early_ref, 2 * block, dot_weight(activated_ref[:, part], cotangent))
    put(early_ref, 8, dot_weight(hidden_three, before_ref[...]))
    early.core_out()
    grad_three = dot_back(before_ref[...], w_up_ref[...])
    grad_norm, grad_gain_ffn = norm_back(grad_three, unit_three, inverse_three, gain_ffn_ref[...])
    grad_after_time = wide(cotangent) + grad_norm

    grad_low = low(grad_after_time)
    put(middle_ref, 6, dot_weight(mixed_two, grad_low))
    grad_mixed = dot_back(grad_low, w_temporal_out_ref[...])

    def over_rounds(value):
        return (value[:64] + value[64:128]) + (value[128:192] + value[192:])

    def put_time(index, grad_key, grad_value):
        grad_packed_ref[index * 64 : index * 64 + 64, WIDTH : 2 * WIDTH] = low(over_rounds(grad_key))
        grad_packed_ref[index * 64 : index * 64 + 64, 2 * WIDTH :] = low(over_rounds(grad_value))

    grad_packed_ref[:, :WIDTH] = low(temporal.backward(time_query, grad_mixed, put_time))
    early.core_in()
    put(middle_ref, 0, dot_weight(hidden_two, grad_packed_ref[...]))
    middle.core_out()
    grad_two = dot_back(grad_packed_ref[...], w_temporal_ref[...])
    grad_norm, grad_gain_time = norm_back(grad_two, unit_two, inverse_two, gain_time_ref[...])
    grad_after_tanner = grad_after_time + grad_norm

    grad_low = low(grad_after_tanner)
    put(late_ref, 6, dot_weight(mixed_one, grad_low))
    grad_mixed = dot_back(grad_low, w_merge_ref[...])

    def put_tanner(index, grad_key, grad_value):
        for grad, part in ((grad_key, slice(0, WIDTH)), (grad_value, slice(WIDTH, 2 * WIDTH))):
            if index == 0:
                own_grad_ref[:, part] = grad
            elif index == 1:
                rows_grad_ref[:, part] = grad
            elif index == 4:
                columns_grad_ref[:, part] = grad
            elif index in (2, 3):
                by = offsets_ref[1, index - 1]
                turned = turn(grad, by)
                own_grad_ref[:, part] += jnp.where(column >= by, turned, 0.0)
                columns_grad_ref[:, part] += jnp.where(column >= by, 0.0, turned)
            else:
                padded_ref[index - 5, :, 8:16, :, part] = grad.reshape(ROUNDS, 8, 8, WIDTH)

    query_low = low(tanner.backward(query, grad_mixed, put_tanner))
    middle.core_in()
    own_grad, rows_grad = own_grad_ref[...], rows_grad_ref[...]
    for index in (5, 6):
        by = offsets_ref[0, index - 1]
        own_grad = own_grad + padded_ref[index - 5, :, pl.ds(8 - by, 8)].reshape(TOKENS, 2 * WIDTH)
        rows_grad = rows_grad + padded_ref[index - 5, :, pl.ds(16 - by, 8)].reshape(TOKENS, 2 * WIDTH)
    rows_low, own_low, columns_low = low(rows_grad), low(own_grad), low(columns_grad_ref[...])
    put(late_ref, 0, dot_weight(hidden_one, query_low))
    put(
        late_ref,
        2,
        dot_weight(hidden_one, own_low)
        + dot_weight(hidden_ref[TOKENS : 2 * TOKENS], rows_low)
        + dot_weight(hidden_ref[2 * TOKENS :], columns_low),
    )
    late.core_out()
    back_out_ref[1] = low(dot_back(columns_low, w_key_value_ref[...]))
    back_columns = send(3, back_out_ref.at[1], back_in_ref.at[1], place.column_tile(1))
    back_out_ref[0] = low(dot_back(rows_low, w_key_value_ref[...]))
    back_rows = send(2, back_out_ref.at[0], back_in_ref.at[0], place.row_tile(1))
    grad_one = dot_back(query_low, w_query_ref[...]) + dot_back(own_low, w_key_value_ref[...])
    late.core_in()
    early.strip_in()
    middle.strip_in()
    back_rows.wait()
    back_columns.wait()
    grad_one = grad_one + (wide(back_in_ref[0]) + wide(back_in_ref[1]))
    grad_norm, grad_gain_tanner = norm_back(grad_one, unit_one, inverse_one, gain_tanner_ref[...])
    grad_embedded = grad_after_tanner + grad_norm
    upper, lower = halves(grad_embedded)
    from_table = dot_weight(features, upper) + dot_weight(features, lower)
    row = iota((SMALL_ROWS, WIDTH), 0)
    shares = jnp.where(row == 9, grad_gain_tanner, from_table)
    shares = jnp.where(row == 10, grad_gain_time, shares)
    shares = jnp.where(row == 11, grad_gain_ffn, shares)
    small.out(0, shares)
    token_grad_ref[...] = upper
    early.plane_in()
    middle.plane_in()
    late.strip_in()
    small.out(1, small.total())
    late.plane_in()
    early.z_in()
    middle.z_in()
    small.out(2, small.total())
    late.z_in()
    early.strip_gathered()
    middle.strip_gathered()
    late.strip_gathered()
    early.plane_gathered()
    middle.plane_gathered()
    late.plane_gathered()
    small_result_ref[...] = small.total()
    early.finish()
    middle.finish()
    late.finish()


def window(*operands):
    vmem = pl.BlockSpec(memory_space=pltpu.VMEM)
    specs = [vmem] * len(operands)
    for index in (7, 8, 9, 11, 12, 14, 15, 16):
        specs[index] = pl.BlockSpec(memory_space=pltpu.HBM)
    bf16, f32 = jnp.bfloat16, jnp.float32
    return pl.pallas_call(
        window_kernel,
        name="window",
        out_shape=(
            jax.ShapeDtypeStruct((RESULT_ROWS, 128), bf16),
            jax.ShapeDtypeStruct((SMALL_ROWS, WIDTH), f32),
            jax.ShapeDtypeStruct((TOKENS, WIDTH), bf16),
        ),
        in_specs=specs,
        out_specs=(vmem, vmem, vmem),
        scratch_shapes=[
            *[pltpu.VMEM(operands[index].shape, bf16) for index in (7, 8, 9, 11, 12, 14, 15, 16)],
            pltpu.SemaphoreType.DMA((8,)),
            pltpu.VMEM((4 * HALF, 128), bf16),
            pltpu.VMEM((2 * HALF, 128), bf16),
            pltpu.VMEM((2 * HALF, 128), bf16),
            pltpu.VMEM((NEIGHBOURS * WIDTH, 128), bf16),
            pltpu.VMEM((256, NEIGHBOURS * WIDTH), bf16),
            pltpu.VMEM((3 * TOKENS, WIDTH), bf16),
            pltpu.VMEM((2, TOKENS, WIDTH), bf16),
            pltpu.VMEM((2, TOKENS, WIDTH), bf16),
            pltpu.VMEM((ROUNDS, 16, 8, 2 * WIDTH), f32),
            pltpu.VMEM((NEIGHBOURS, TOKENS, 2 * WIDTH), f32),
            pltpu.VMEM((2, ROUNDS, 24, 8, 2 * WIDTH), f32),
            pltpu.VMEM((TOKENS, 2 * WIDTH), f32),
            pltpu.VMEM((TOKENS, 2 * WIDTH), f32),
            pltpu.VMEM((TOKENS, 2 * WIDTH), f32),
            pltpu.VMEM((TOKENS, FF), bf16),
            pltpu.VMEM((TOKENS, FF), bf16),
            pltpu.VMEM((TOKENS, 3 * WIDTH), f32),
            pltpu.VMEM((TOKENS, 3 * WIDTH), bf16),
            pltpu.SemaphoreType.DMA((4,)),
            pltpu.SemaphoreType.DMA((4,)),
            *SmallSum.SCRATCH,
            *TwoStepSum.scratch(2 * HALF),
            *TwoStepSum.scratch(HALF),
            *TwoStepSum.scratch(HALF),
        ],
        compiler_params=pltpu.CompilerParams(
            collective_id=0, has_side_effects=True, vmem_limit_bytes=36 * 2**20),
    )(*[pltpu.with_memory_space_constraint(x, pltpu.HBM) for x in operands])


def finish_kernel(scale, slabs_ref, small_ref, token_grad_in_ref, *outs):
    (token_grad_ref, flip_ref, plan_ref, gain_tanner_ref, query_ref, key_value_ref, merge_ref,
     gain_time_ref, temporal_ref, temporal_out_ref, gain_ffn_ref, up_ref, down_ref) = outs
    token_grad_ref[...] = token_grad_in_ref[...]
    small = small_ref[...] * scale
    plan_ref[...] = small[:8]
    flip_ref[...] = small[8:9]
    gain_tanner_ref[...] = small[9:10]
    gain_time_ref[...] = small[10:11]
    gain_ffn_ref[...] = small[11:12]

    def take(target, slab):
        for block in range(target.shape[0] // 256):
            for half in range(target.shape[1] // 128):
                target[block * 256 : block * 256 + 256, half * 128 : half * 128 + 128] = (
                    wide(slabs_ref[slab * 256 : slab * 256 + 256]) * scale)
                slab += 1

    take(down_ref, 0)
    take(up_ref, 8)
    take(temporal_ref, 16)
    take(temporal_out_ref, 22)
    take(query_ref, 24)
    take(key_value_ref, 26)
    take(merge_ref, 30)


def finish(scale, slabs, small, token_grad):
    vmem = pl.BlockSpec(memory_space=pltpu.VMEM)
    f32 = jnp.float32
    return pl.pallas_call(
        lambda *refs: finish_kernel(scale, *refs),
        name="finish",
        out_shape=(
            jax.ShapeDtypeStruct((TOKENS, WIDTH), jnp.bfloat16),
            jax.ShapeDtypeStruct((1, WIDTH), f32),
            jax.ShapeDtypeStruct((PLAN_STEP_COUNT, WIDTH), f32),
            jax.ShapeDtypeStruct((1, WIDTH), f32),
            jax.ShapeDtypeStruct((WIDTH, WIDTH), f32),
            jax.ShapeDtypeStruct((WIDTH, 2 * WIDTH), f32),
            jax.ShapeDtypeStruct((WIDTH, WIDTH), f32),
            jax.ShapeDtypeStruct((1, WIDTH), f32),
            jax.ShapeDtypeStruct((WIDTH, 3 * WIDTH), f32),
            jax.ShapeDtypeStruct((WIDTH, WIDTH), f32),
            jax.ShapeDtypeStruct((1, WIDTH), f32),
            jax.ShapeDtypeStruct((WIDTH, FF), f32),
            jax.ShapeDtypeStruct((FF, WIDTH), f32),
        ),
        in_specs=[vmem] * 3,
        out_specs=(vmem,) * 13,
        compiler_params=pltpu.CompilerParams(vmem_limit_bytes=32 * 2**20),
    )(slabs, small, token_grad)


def on_device(
    tokens,
    syndrome,
    check_plan_step,
    offsets,
    flip_vector,
    plan_step_embedding,
    gain_tanner,
    w_query,
    w_key_value,
    w_merge,
    gain_time,
    w_temporal,
    w_temporal_out,
    gain_ffn,
    w_ffn_up,
    w_ffn_down,
    cotangent,
):
    tile = tokens.shape
    devices = lax.axis_size("gx") * lax.axis_size("gy")
    scale = 1.0 / math.sqrt(tile[0] * tile[1] * tile[2] * devices)
    slabs, small, token_grad = window(
        tokens.reshape(TOKENS, WIDTH),
        syndrome.reshape(TOKENS // 8, 8),
        check_plan_step.reshape(TOKENS // 8, 8),
        offsets.T,
        flip_vector.reshape(1, WIDTH),
        plan_step_embedding,
        gain_tanner.reshape(1, WIDTH),
        w_query,
        w_key_value,
        w_merge,
        gain_time.reshape(1, WIDTH),
        w_temporal,
        w_temporal_out,
        gain_ffn.reshape(1, WIDTH),
        w_ffn_up,
        w_ffn_down,
        cotangent.reshape(TOKENS, WIDTH),
    )
    outs = list(finish(scale, slabs, small, token_grad))
    outs[0] = outs[0].reshape(tile)
    for index in (1, 3, 7, 10):
        outs[index] = outs[index].reshape(WIDTH)
    return tuple(outs)


def solution(mesh):
    return jax.shard_map(
        on_device,
        mesh=mesh,
        in_specs=(
            P(None, "gx", "gy", None),
            P(None, "gx", "gy"),
            P(None, "gx", "gy"),
            P(),
            P(),
            P(),
            P(),
            P(),
            P(),
            P(),
            P(),
            P(),
            P(),
            P(),
            P(),
            P(),
            P(None, "gx", "gy", None),
        ),
        out_specs=(
            P(None, "gx", "gy", None),
            P(),
            P(),
            P(),
            P(),
            P(),
            P(),
            P(),
            P(),
            P(),
            P(),
            P(),
            P(),
        ),
        check_vma=False,
    )
```

```python
import math

import jax
import jax.numpy as jnp
from jax import lax
from jax.experimental import pallas as pl
from jax.experimental.pallas import tpu as pltpu
from jax.sharding import PartitionSpec as P

WIDTH = 256
HEADDIM = 32
FF = 1024
PLAN_STEP_COUNT = 8
TOKENS = 256
NEIGHBOURS = 7
ROUNDS = 4
EPS = 1e-05
CAP = 4.0
ROOT = math.sqrt(HEADDIM)
GELU = math.sqrt(2 / math.pi)

MESH = pl.DeviceIdType.MESH
HALF = 1024
RESULT_ROWS = 8 * HALF
PLANE_STEPS = sorted(
    [(x, y) for x in range(4) for y in range(4) if x or y], key=lambda at: -(at[0] % 2 + at[1] % 2 + 2 * (at[0] == 2) + 2 * (at[1] == 2)))
Z_STEPS = (4, 3, 5, 2, 6, 1, 7)
SMALL_ROWS = 16


class Place:
    def __init__(self):
        self.gx = lax.axis_index("gx")
        self.gy = lax.axis_index("gy")
        self.z = lax.rem(self.gx, 8)
        self.y_lo = lax.div(self.gx, 8)
        self.core = lax.rem(self.gy, 2)
        self.y_hi = lax.rem(lax.div(self.gy, 2), 2)
        self.x = lax.div(self.gy, 4)
        self.y = self.y_hi * 2 + self.y_lo

    def other_core(self):
        return (self.gx, self.gy + 1 - 2 * self.core)

    def at_x(self, x):
        return (self.gx, x * 4 + self.y_hi * 2 + self.core)

    def at_y(self, y):
        return (lax.rem(y, 2) * 8 + self.z, self.x * 4 + lax.div(y, 2) * 2 + self.core)

    def in_plane(self, x, y):
        return (lax.rem(y, 2) * 8 + self.z, x * 4 + lax.div(y, 2) * 2 + self.core)

    def at_z(self, z):
        return (self.y_lo * 8 + z, self.gy)

    def greeted(self):
        peers = [self.row_tile(1), self.column_tile(1), self.row_tile(15), self.column_tile(15)]
        peers.append(self.other_core())
        for step_x, step_y in PLANE_STEPS:
            peers.append(self.in_plane(lax.rem(self.x + step_x, 4), lax.rem(self.y + step_y, 4)))
        for step in range(1, 8):
            peers.append(self.at_z(lax.rem(self.z + step, 8)))
        return peers

    def row_tile(self, step):
        return (lax.rem(self.gx + step, 16), self.gy)

    def column_tile(self, step):
        return (self.gx, lax.rem(self.gy + step, 16))


def greet(peers):
    barrier = pltpu.get_barrier_semaphore()
    for peer in peers:
        pl.semaphore_signal(barrier, inc=1, device_id=peer, device_id_type=MESH)
    return barrier, len(peers)


def rows(start, count):
    return pl.ds(pl.multiple_of(start, min(count, 16)), count)


class Sum:
    @staticmethod
    def scratch(half):
        bf16 = jnp.bfloat16
        return (
            pltpu.VMEM((half, 128), bf16),
            pltpu.VMEM((half, 128), bf16),
            pltpu.VMEM((15, half // 16, 128), bf16),
            pltpu.VMEM((8, half // 16, 128), bf16),
            pltpu.SemaphoreType.DMA((54,)),
            pltpu.SemaphoreType.DMA((54,)),
        )

    def __init__(self, place, half, base, source, result, scratch):
        self.place = place
        self.half = half
        self.chunk = half // 16
        self.base = base + place.core * half
        self.source = source
        self.result = result
        self.from_core, self.one, self.in_two, self.along_z, self.send, self.recv = scratch

    def copy(self, slot, source, target, peer):
        copy = pltpu.make_async_remote_copy(
            src_ref=source,
            dst_ref=target,
            send_sem=self.send.at[slot],
            recv_sem=self.recv.at[slot],
            device_id=peer,
            device_id_type=MESH,
        )
        copy.start()
        return copy

    def to_plane(self, slot, source, target):
        p = self.place
        self.copies = []
        for index, (step_x, step_y) in enumerate(PLANE_STEPS):
            x, y = lax.rem(p.x + step_x, 4), lax.rem(p.y + step_y, 4)
            self.copies.append(
                self.copy(slot + index, source((x * 4 + y) * self.chunk), target(index), p.in_plane(x, y)))

    def in_result(self, x, y):
        return self.result.at[rows(self.base + (x * 4 + y) * self.chunk, self.chunk)]

    def core_out(self):
        other = rows((1 - self.place.core) * self.half, self.half)
        self.core_copy = self.copy(0, self.source.at[other], self.from_core, self.place.other_core())

    def core_in(self):
        self.core_copy.wait()
        own = self.source[rows(self.place.core * self.half, self.half)]
        self.one[...] = (own.astype(jnp.float32) + self.from_core[...].astype(jnp.float32)).astype(jnp.bfloat16)
        self.to_plane(
            1, lambda at: self.one.at[rows(at, self.chunk)], lambda index: self.in_two.at[index])

    def plane_in(self):
        p = self.place
        for copy in self.copies:
            copy.wait()
        total = self.one[rows((p.x * 4 + p.y) * self.chunk, self.chunk)].astype(jnp.float32)
        for index in range(15):
            total = total + self.in_two[index].astype(jnp.float32)
        self.along_z[p.z] = total.astype(jnp.bfloat16)
        own = self.along_z.at[p.z]
        self.copies = []
        for index, step in enumerate(Z_STEPS):
            self.copies.append(self.copy(16 + index, own, own, p.at_z(lax.rem(p.z + step, 8))))

    def z_in(self):
        p = self.place
        for copy in self.copies:
            copy.wait()
        total = self.along_z[0].astype(jnp.float32)
        for index in range(1, 8):
            total = total + self.along_z[index].astype(jnp.float32)
        self.result[rows(self.base + (p.x * 4 + p.y) * self.chunk, self.chunk)] = total.astype(jnp.bfloat16)
        own = self.in_result(p.x, p.y)
        self.to_plane(23, lambda at: own, lambda index: own)
        self.core_copies = [self.copy(38, own, own, p.other_core())]

    def plane_gathered(self):
        p = self.place
        for index in reversed(range(15)):
            self.copies[index].wait()
            step_x, step_y = PLANE_STEPS[index]
            chunk = self.in_result(lax.rem(p.x + 4 - step_x, 4), lax.rem(p.y + 4 - step_y, 4))
            self.core_copies.append(self.copy(39 + index, chunk, chunk, p.other_core()))

    def finish(self):
        for copy in self.core_copies:
            copy.wait()


class TwoStepSum(Sum):
    @staticmethod
    def scratch(half):
        bf16 = jnp.bfloat16
        return (
            pltpu.VMEM((half, 128), bf16),
            pltpu.VMEM((half, 128), bf16),
            pltpu.VMEM((6, half // 8, 128), bf16),
            pltpu.VMEM((2, half // 8, 128), bf16),
            pltpu.VMEM((6, half // 32, 128), bf16),
            pltpu.VMEM((8, half // 16, 128), bf16),
            pltpu.SemaphoreType.DMA((40,)),
            pltpu.SemaphoreType.DMA((40,)),
        )

    def __init__(self, place, half, base, source, result, scratch):
        self.place = place
        self.half = half
        self.strip = half // 8
        self.chunk = half // 32
        self.base = base + place.core * half
        self.source = source
        self.result = result
        (self.from_core, self.one, self.in_one, self.two, self.in_two, self.along_z, self.send, self.recv) = scratch

    def both_ways(self, slot, first_along_x, first, second, first_target, second_target):
        p = self.place
        self.copies = []
        for index, step in enumerate((2, 1, 3)):
            x, y = lax.rem(p.x + step, 4), lax.rem(p.y + step, 4)
            of_first, of_second = ((x, p.at_x(x)), (y, p.at_y(y)))[:: 1 if first_along_x else -1]
            self.copies.append(
                self.copy(slot + index, first(of_first[0]), first_target(index), of_first[1]))
            self.copies.append(
                self.copy(slot + 3 + index, second(of_second[0]), second_target(index), of_second[1]))

    def core_in(self):
        self.core_copy.wait()
        own = self.source[rows(self.place.core * self.half, self.half)]
        self.one[...] = (own.astype(jnp.float32) + self.from_core[...].astype(jnp.float32)).astype(jnp.bfloat16)
        middle = self.half // 2
        self.both_ways(
            1,
            True,
            lambda x: self.one.at[rows(x * self.strip, self.strip)],
            lambda y: self.one.at[rows(middle + y * self.strip, self.strip)],
            lambda index: self.in_one.at[index],
            lambda index: self.in_one.at[3 + index],
        )

    def strip_in(self):
        p = self.place
        for copy in self.copies:
            copy.wait()
        for part, own in ((0, p.x * self.strip), (1, self.half // 2 + p.y * self.strip)):
            total = self.one[rows(own, self.strip)].astype(jnp.float32)
            for index in range(3):
                total = total + self.in_one[part * 3 + index].astype(jnp.float32)
            self.two[part] = total.astype(jnp.bfloat16)
        self.both_ways(
            7,
            False,
            lambda y: self.two.at[0, rows(y * self.chunk, self.chunk)],
            lambda x: self.two.at[1, rows(x * self.chunk, self.chunk)],
            lambda index: self.in_two.at[index],
            lambda index: self.in_two.at[3 + index],
        )

    def plane_in(self):
        p = self.place
        for copy in self.copies:
            copy.wait()
        for part, own in ((0, p.y * self.chunk), (1, p.x * self.chunk)):
            total = self.two[part, rows(own, self.chunk)].astype(jnp.float32)
            for index in range(3):
                total = total + self.in_two[part * 3 + index].astype(jnp.float32)
            self.along_z[p.z, part * self.chunk : (part + 1) * self.chunk] = total.astype(jnp.bfloat16)
        own = self.along_z.at[p.z]
        self.copies = []
        for index, step in enumerate(Z_STEPS):
            self.copies.append(self.copy(13 + index, own, own, p.at_z(lax.rem(p.z + step, 8))))

    def z_in(self):
        p = self.place
        for copy in self.copies:
            copy.wait()
        total = self.z_total()
        first = rows(self.base + p.x * self.strip + p.y * self.chunk, self.chunk)
        second = rows(self.base + self.half // 2 + p.y * self.strip + p.x * self.chunk, self.chunk)
        self.result[first] = total[: self.chunk]
        self.result[second] = total[self.chunk :]
        first, second = self.result.at[first], self.result.at[second]
        self.both_ways(
            20, False, lambda _: first, lambda _: second, lambda _: first, lambda _: second)

    def strip_of(self, part, index):
        return self.result.at[rows(self.base + part * (self.half // 2) + index * self.strip, self.strip)]

    def strip_gathered(self):
        p = self.place
        for copy in self.copies:
            copy.wait()
        first, second = self.strip_of(0, p.x), self.strip_of(1, p.y)
        self.both_ways(
            26, True, lambda _: first, lambda _: second, lambda _: first, lambda _: second)
        self.core_copies = [
            self.copy(32, first, first, p.other_core()), self.copy(33, second, second, p.other_core())]

    def plane_gathered(self):
        p = self.place
        for index in reversed(range(6)):
            self.copies[index].wait()
            part, step = index % 2, (2, 1, 3)[index // 2]
            strip = self.strip_of(part, lax.rem((p.x, p.y)[part] + 4 - step, 4))
            self.core_copies.append(self.copy(34 + index, strip, strip, p.other_core()))

    def z_total(self):
        total = self.along_z[0].astype(jnp.float32)
        for index in range(1, 8):
            total = total + self.along_z[index].astype(jnp.float32)
        return total.astype(jnp.bfloat16)


class ThreeStepSum(TwoStepSum):
    @staticmethod
    def scratch(half):
        bf16 = jnp.bfloat16
        return (
            *TwoStepSum.scratch(half)[:5],
            pltpu.VMEM((2, half // 16, 128), bf16),
            pltpu.SemaphoreType.DMA((47,)),
            pltpu.SemaphoreType.DMA((47,)),
            pltpu.VMEM((7, half // 128, 128), bf16),
        )

    def __init__(self, place, half, base, source, result, scratch):
        super().__init__(place, half, base, source, result, scratch[:8])
        self.in_z = scratch[8]
        self.part = half // 128

    def plane_in(self):
        p = self.place
        for copy in self.copies:
            copy.wait()
        for part, own in ((0, p.y * self.chunk), (1, p.x * self.chunk)):
            total = self.two[part, rows(own, self.chunk)].astype(jnp.float32)
            for index in range(3):
                total = total + self.in_two[part * 3 + index].astype(jnp.float32)
            self.along_z[0, part * self.chunk : (part + 1) * self.chunk] = total.astype(jnp.bfloat16)
        self.copies = []
        for index, step in enumerate(Z_STEPS):
            z = lax.rem(p.z + step, 8)
            share = self.along_z.at[0, rows(z * self.part, self.part)]
            self.copies.append(self.copy(13 + index, share, self.in_z.at[index], p.at_z(z)))

    def part_in(self):
        p = self.place
        for copy in self.copies:
            copy.wait()
        own = rows(p.z * self.part, self.part)
        total = self.along_z[0, own].astype(jnp.float32)
        for index in range(7):
            total = total + self.in_z[index].astype(jnp.float32)
        self.along_z[1, own] = total.astype(jnp.bfloat16)
        share = self.along_z.at[1, own]
        self.copies = []
        for index, step in enumerate(Z_STEPS):
            self.copies.append(self.copy(40 + index, share, share, p.at_z(lax.rem(p.z + step, 8))))

    def z_total(self):
        return self.along_z[1]


class SmallSum:
    SCRATCH = (
        pltpu.VMEM((2, SMALL_ROWS, 256), jnp.bfloat16),
        pltpu.VMEM((4, SMALL_ROWS, 256), jnp.bfloat16),
        pltpu.VMEM((4, SMALL_ROWS, 256), jnp.bfloat16),
        pltpu.VMEM((8, SMALL_ROWS, 256), jnp.bfloat16),
        pltpu.SemaphoreType.DMA((14,)),
        pltpu.SemaphoreType.DMA((14,)),
    )

    def __init__(self, place, scratch):
        self.place = place
        self.slots = scratch[:4]
        self.send, self.recv = scratch[4:]

    def out(self, stage, value):
        p = self.place
        self.stage = stage
        slots = self.slots[stage]
        mine = (p.core, p.x, p.y, p.z)[stage]
        if stage == 0:
            peers = [p.other_core()]
        elif stage == 1:
            peers = [p.at_x(lax.rem(p.x + step, 4)) for step in (2, 1, 3)]
        elif stage == 2:
            peers = [p.at_y(lax.rem(p.y + step, 4)) for step in (2, 1, 3)]
        else:
            peers = [p.at_z(lax.rem(p.z + step, 8)) for step in Z_STEPS]
        slots[mine] = value.astype(jnp.bfloat16)
        self.copies = []
        for index, peer in enumerate(peers):
            copy = pltpu.make_async_remote_copy(
                src_ref=slots.at[mine],
                dst_ref=slots.at[mine],
                send_sem=self.send.at[(0, 1, 4, 7)[stage] + index],
                recv_sem=self.recv.at[(0, 1, 4, 7)[stage] + index],
                device_id=peer,
                device_id_type=MESH,
            )
            copy.start()
            self.copies.append(copy)

    def total(self):
        for copy in self.copies:
            copy.wait()
        slots = self.slots[self.stage]
        total = slots[0].astype(jnp.float32)
        for index in range(1, slots.shape[0]):
            total = total + slots[index].astype(jnp.float32)
        return total


def dot(left, right):
    return lax.dot_general(left, right, (((1,), (0,)), ((), ())), preferred_element_type=jnp.float32)


def dot_back(grad, weight):
    return lax.dot_general(grad, weight, (((1,), (1,)), ((), ())), preferred_element_type=jnp.float32)


def dot_weight(inputs, grad):
    return lax.dot_general(inputs, grad, (((0,), (0,)), ((), ())), preferred_element_type=jnp.float32)


def low(value):
    return value.astype(jnp.bfloat16)


def wide(value):
    return value.astype(jnp.float32)


def halves(value):
    upper = low(value)
    return upper, low(value - wide(upper))


def ones(mask):
    return low(jnp.where(mask, 1.0, 0.0))


def iota(shape, axis):
    return lax.broadcasted_iota(jnp.int32, shape, axis)


def norm(stream, gain):
    inverse = lax.rsqrt(jnp.mean(stream * stream, axis=-1, keepdims=True) + EPS)
    unit = stream * inverse
    return unit, inverse, low(unit * gain)


def norm_back(grad, unit, inverse, gain):
    scaled = grad * gain
    along = jnp.mean(scaled * unit, axis=-1, keepdims=True)
    return inverse * (scaled - unit * along), jnp.sum(grad * unit, axis=0, keepdims=True)


def over_neighbours(value):
    value = value + pltpu.roll(value, 64, 1)
    value = value + pltpu.roll(value, 32, 1)
    return value + pltpu.roll(value, 16, 1)


class Attention:
    def __init__(self, gather_ref, spread_ref, order, key, value, allowed):
        self.gather_ref = gather_ref
        self.spread_ref = spread_ref
        self.count = len(order)
        self.order = order
        self.key = key
        self.value = value
        self.allowed = allowed

    def gather(self, products):
        total = jnp.zeros((TOKENS, 128), jnp.float32)
        for index in range(self.count):
            matrix = self.gather_ref[index * WIDTH : (index + 1) * WIDTH]
            upper, lower = halves(products(index))
            total = total + dot(upper, matrix) + dot(lower, matrix)
        return total

    def spread(self, small, index):
        both = jnp.concatenate(halves(small), axis=1)
        return dot(both, self.spread_ref[:, index * WIDTH : (index + 1) * WIDTH])

    def forward(self, query):
        score = self.gather(lambda index: query * self.key(index))
        self.capped = jnp.tanh(score * (1.0 / (ROOT * CAP)))
        weight = jnp.where(self.allowed, jnp.exp(CAP * self.capped), 0.0)
        self.share = weight / over_neighbours(weight)
        mixed = jnp.zeros((TOKENS, WIDTH), jnp.float32)
        for index in range(self.count):
            mixed = mixed + self.spread(self.share, index) * self.value(index)
        return mixed

    def backward(self, query, grad, put):
        grad_share = self.gather(lambda index: grad * self.value(index))
        along = over_neighbours(self.share * grad_share)
        grad_score = self.share * (grad_share - along) * (1.0 - self.capped * self.capped) * (1.0 / ROOT)
        grad_query = jnp.zeros((TOKENS, WIDTH), jnp.float32)
        for index in self.order:
            spread = self.spread(grad_score, index)
            grad_query = grad_query + spread * self.key(index)
            put(index, spread * query, self.spread(self.share, index) * grad)
        return grad_query


def turn(value, by):
    return pltpu.roll(value.reshape(TOKENS // 8, 8, -1), by, 1).reshape(TOKENS, -1)


def window_kernel(
    tokens_ref,
    syndrome_ref,
    step_ref,
    offsets_ref,
    flip_ref,
    embedding_ref,
    gain_tanner_ref,
    w_query_hbm,
    w_key_value_hbm,
    w_merge_hbm,
    gain_time_ref,
    w_temporal_hbm,
    w_temporal_out_hbm,
    gain_ffn_ref,
    w_up_hbm,
    w_down_hbm,
    cotangent_hbm,
    result_ref,
    small_result_ref,
    token_grad_ref,
    w_query_ref,
    w_key_value_ref,
    w_merge_ref,
    w_temporal_ref,
    w_temporal_out_ref,
    w_up_ref,
    w_down_ref,
    cotangent_ref,
    loaded,
    early_ref,
    middle_ref,
    late_ref,
    gather_ref,
    spread_ref,
    hidden_ref,
    back_out_ref,
    back_in_ref,
    ahead_ref,
    near_ref,
    padded_ref,
    own_grad_ref,
    rows_grad_ref,
    columns_grad_ref,
    activated_ref,
    before_ref,
    packed_ref,
    grad_packed_ref,
    halo_send,
    halo_recv,
    *scratch,
):
    place = Place()
    barrier, greeted = greet(place.greeted())
    loads = []
    for index, (source, target) in enumerate((
        (w_query_hbm, w_query_ref),
        (w_key_value_hbm, w_key_value_ref),
        (w_merge_hbm, w_merge_ref),
        (w_temporal_hbm, w_temporal_ref),
        (w_temporal_out_hbm, w_temporal_out_ref),
        (w_up_hbm, w_up_ref),
        (w_down_hbm, w_down_ref),
        (cotangent_hbm, cotangent_ref),
    )):
        load = pltpu.make_async_copy(source, target, loaded.at[index])
        load.start()
        loads.append(load)
    groups = ((ThreeStepSum, 2 * HALF, 0, early_ref), (TwoStepSum, HALF, 4 * HALF, middle_ref), (TwoStepSum, HALF, 6 * HALF, late_ref))
    ends = [len(SmallSum.SCRATCH)]
    for kind, half, _, _ in groups:
        ends.append(ends[-1] + len(kind.scratch(half)))
    early, middle, late = (
        kind(place, half, base, source, result_ref, scratch[ends[index] : ends[index + 1]])
        for index, (kind, half, base, source) in enumerate(groups))
    small = SmallSum(place, scratch[: ends[0]])

    def send(slot, source, target, peer):
        copy = pltpu.make_async_remote_copy(
            src_ref=source,
            dst_ref=target,
            send_sem=halo_send.at[slot],
            recv_sem=halo_recv.at[slot],
            device_id=peer,
            device_id_type=MESH,
        )
        copy.start()
        return copy

    code = low(wide(step_ref[...] + 16 * syndrome_ref[...]))
    site_row = ones(lax.div(iota((TOKENS, 32), 0), 8) == iota((TOKENS, 32), 1))
    site_column = lax.rem(iota((TOKENS, 8), 0), 8) == iota((TOKENS, 8), 1)
    code = jnp.sum(jnp.where(site_column, dot(site_row, code), 0.0), axis=1, keepdims=True)
    lane = iota((TOKENS, 16), 1)
    lane_value = wide(lane)
    flipped = jnp.where(code > 15.5, 1.0, 0.0)
    on_step = jnp.where(code - 16.0 * flipped == lane_value, 1.0, 0.0)
    features = low(jnp.where(lane < 8, on_step, jnp.where(lane == 8, flipped, 0.0)))
    table = jnp.concatenate(
        [embedding_ref[...], jnp.broadcast_to(flip_ref[...], (8, WIDTH))], axis=0)
    upper = low(table)
    next_upper, lower = halves(table - wide(upper))
    embedded = wide(tokens_ref[...]) + (dot(features, upper) + (dot(features, next_upper) + dot(features, lower)))
    unit_one, inverse_one, hidden_one = norm(embedded, gain_tanner_ref[...])
    hidden_ref[:TOKENS] = hidden_one
    pl.semaphore_wait(barrier, greeted)
    own_hidden = hidden_ref.at[pl.ds(0, TOKENS)]
    ahead_rows = send(0, own_hidden, hidden_ref.at[pl.ds(TOKENS, TOKENS)], place.row_tile(15))
    ahead_columns = send(1, own_hidden, hidden_ref.at[pl.ds(2 * TOKENS, TOKENS)], place.column_tile(15))

    for index in range(2):
        padded_ref[index, :, 0:8] = jnp.zeros((ROUNDS, 8, 8, 2 * WIDTH), jnp.float32)
        padded_ref[index, :, 16:24] = jnp.zeros((ROUNDS, 8, 8, 2 * WIDTH), jnp.float32)

    shape = (NEIGHBOURS * WIDTH, 128)
    feature = iota(shape, 0)
    gather_ref[...] = ones(
        lax.div(feature, WIDTH) * 16 + lax.div(lax.rem(feature, WIDTH), HEADDIM) == iota(shape, 1))
    shape = (256, NEIGHBOURS * WIDTH)
    feature = iota(shape, 1)
    spread_ref[...] = ones(
        lax.div(feature, WIDTH) * 16 + lax.div(lax.rem(feature, WIDTH), HEADDIM) == lax.rem(iota(shape, 0), 128))

    for load in loads[:3]:
        load.wait()
    query = wide(low(dot(hidden_one, w_query_ref[...])))
    own = wide(low(dot(hidden_one, w_key_value_ref[...])))
    near_ref[0] = own
    ahead_ref[:, 0:8] = own.reshape(ROUNDS, 8, 8, 2 * WIDTH)
    ahead_rows.wait()
    rows_ahead = wide(low(dot(hidden_ref[TOKENS : 2 * TOKENS], w_key_value_ref[...])))
    near_ref[1] = rows_ahead
    ahead_ref[:, 8:16] = rows_ahead.reshape(ROUNDS, 8, 8, 2 * WIDTH)
    for index in (5, 6):
        near_ref[index] = ahead_ref[:, pl.ds(offsets_ref[0, index - 1], 8)].reshape(TOKENS, 2 * WIDTH)
    ahead_columns.wait()
    columns_ahead = wide(low(dot(hidden_ref[2 * TOKENS :], w_key_value_ref[...])))
    near_ref[4] = columns_ahead
    column = lax.rem(iota((TOKENS, 1), 0), 8)
    for index in (2, 3):
        by = offsets_ref[1, index - 1]
        near_ref[index] = jnp.where(column < 8 - by, turn(own, 8 - by), turn(columns_ahead, 8 - by))
    lanes = iota((TOKENS, 128), 1)
    tanner = Attention(
        gather_ref,
        spread_ref,
        (0, 1, 4, 2, 3, 5, 6),
        lambda index: near_ref[index, :, :WIDTH],
        lambda index: near_ref[index, :, WIDTH:],
        lanes < NEIGHBOURS * 16,
    )
    mixed_one = low(tanner.forward(query))
    after_tanner = embedded + dot(mixed_one, w_merge_ref[...])

    for load in loads[3:]:
        load.wait()
    unit_two, inverse_two, hidden_two = norm(after_tanner, gain_time_ref[...])
    packed_ref[...] = wide(low(dot(hidden_two, w_temporal_ref[...])))
    time_query = packed_ref[:, :WIDTH]

    def of_round(index, column):
        value = packed_ref[index * 64 : index * 64 + 64, column : column + WIDTH]
        return jnp.concatenate([value] * ROUNDS, axis=0)

    temporal = Attention(
        gather_ref,
        spread_ref,
        (0, 1, 2, 3),
        lambda index: of_round(index, WIDTH),
        lambda index: of_round(index, 2 * WIDTH),
        lax.div(lanes, 16) <= lax.div(iota((TOKENS, 128), 0), 64),
    )
    mixed_two = low(temporal.forward(time_query))
    after_time = after_tanner + dot(mixed_two, w_temporal_out_ref[...])

    def put(target, slab, value):
        for half in range(value.shape[1] // 128):
            target[(slab + half) * 256 : (slab + half + 1) * 256] = low(value[:, half * 128 : half * 128 + 128])

    unit_three, inverse_three, hidden_three = norm(after_time, gain_ffn_ref[...])
    cotangent = cotangent_ref[...]
    for block in range(FF // WIDTH):
        part = slice(block * WIDTH, (block + 1) * WIDTH)
        before = dot(hidden_three, w_up_ref[:, part])
        square = before * before
        bend = jnp.tanh(GELU * before * (1.0 + 0.044715 * square))
        activated_ref[:, part] = low(0.5 * before * (1.0 + bend))
        slope = 0.5 * (1.0 + bend) + 0.5 * before * (1.0 - bend * bend) * (GELU * (1.0 + 3 * 0.044715 * square))
        before_ref[:, part] = low(dot_back(cotangent, w_down_ref[part]) * slope)
    for block in range(FF // WIDTH):
        part = slice(block * WIDTH, (block + 1) * WIDTH)
        put(early_ref, 2 * block, dot_weight(activated_ref[:, part], cotangent))
    put(early_ref, 8, dot_weight(hidden_three, before_ref[...]))
    early.core_out()
    grad_three = dot_back(before_ref[...], w_up_ref[...])
    grad_norm, grad_gain_ffn = norm_back(grad_three, unit_three, inverse_three, gain_ffn_ref[...])
    grad_after_time = wide(cotangent) + grad_norm

    grad_low = low(grad_after_time)
    put(middle_ref, 6, dot_weight(mixed_two, grad_low))
    grad_mixed = dot_back(grad_low, w_temporal_out_ref[...])

    def over_rounds(value):
        return (value[:64] + value[64:128]) + (value[128:192] + value[192:])

    def put_time(index, grad_key, grad_value):
        grad_packed_ref[index * 64 : index * 64 + 64, WIDTH : 2 * WIDTH] = low(over_rounds(grad_key))
        grad_packed_ref[index * 64 : index * 64 + 64, 2 * WIDTH :] = low(over_rounds(grad_value))

    grad_packed_ref[:, :WIDTH] = low(temporal.backward(time_query, grad_mixed, put_time))
    early.core_in()
    put(middle_ref, 0, dot_weight(hidden_two, grad_packed_ref[...]))
    middle.core_out()
    grad_two = dot_back(grad_packed_ref[...], w_temporal_ref[...])
    grad_norm, grad_gain_time = norm_back(grad_two, unit_two, inverse_two, gain_time_ref[...])
    grad_after_tanner = grad_after_time + grad_norm

    grad_low = low(grad_after_tanner)
    put(late_ref, 6, dot_weight(mixed_one, grad_low))
    grad_mixed = dot_back(grad_low, w_merge_ref[...])

    def put_tanner(index, grad_key, grad_value):
        for grad, part in ((grad_key, slice(0, WIDTH)), (grad_value, slice(WIDTH, 2 * WIDTH))):
            if index == 0:
                own_grad_ref[:, part] = grad
            elif index == 1:
                rows_grad_ref[:, part] = grad
            elif index == 4:
                columns_grad_ref[:, part] = grad
            elif index in (2, 3):
                by = offsets_ref[1, index - 1]
                turned = turn(grad, by)
                own_grad_ref[:, part] += jnp.where(column >= by, turned, 0.0)
                columns_grad_ref[:, part] += jnp.where(column >= by, 0.0, turned)
            else:
                padded_ref[index - 5, :, 8:16, :, part] = grad.reshape(ROUNDS, 8, 8, WIDTH)

    query_low = low(tanner.backward(query, grad_mixed, put_tanner))
    middle.core_in()
    own_grad, rows_grad = own_grad_ref[...], rows_grad_ref[...]
    for index in (5, 6):
        by = offsets_ref[0, index - 1]
        own_grad = own_grad + padded_ref[index - 5, :, pl.ds(8 - by, 8)].reshape(TOKENS, 2 * WIDTH)
        rows_grad = rows_grad + padded_ref[index - 5, :, pl.ds(16 - by, 8)].reshape(TOKENS, 2 * WIDTH)
    rows_low, own_low, columns_low = low(rows_grad), low(own_grad), low(columns_grad_ref[...])
    put(late_ref, 0, dot_weight(hidden_one, query_low))
    put(
        late_ref,
        2,
        dot_weight(hidden_one, own_low)
        + dot_weight(hidden_ref[TOKENS : 2 * TOKENS], rows_low)
        + dot_weight(hidden_ref[2 * TOKENS :], columns_low),
    )
    late.core_out()
    back_out_ref[1] = low(dot_back(columns_low, w_key_value_ref[...]))
    back_columns = send(3, back_out_ref.at[1], back_in_ref.at[1], place.column_tile(1))
    back_out_ref[0] = low(dot_back(rows_low, w_key_value_ref[...]))
    back_rows = send(2, back_out_ref.at[0], back_in_ref.at[0], place.row_tile(1))
    grad_one = dot_back(query_low, w_query_ref[...]) + dot_back(own_low, w_key_value_ref[...])
    late.core_in()
    early.strip_in()
    middle.strip_in()
    late.strip_in()
    early.plane_in()
    back_rows.wait()
    back_columns.wait()
    grad_one = grad_one + (wide(back_in_ref[0]) + wide(back_in_ref[1]))
    grad_norm, grad_gain_tanner = norm_back(grad_one, unit_one, inverse_one, gain_tanner_ref[...])
    grad_embedded = grad_after_tanner + grad_norm
    upper, lower = halves(grad_embedded)
    from_table = dot_weight(features, upper) + dot_weight(features, lower)
    row = iota((SMALL_ROWS, WIDTH), 0)
    shares = jnp.where(row == 9, grad_gain_tanner, from_table)
    shares = jnp.where(row == 10, grad_gain_time, shares)
    shares = jnp.where(row == 11, grad_gain_ffn, shares)
    small.out(0, shares)
    token_grad_ref[...] = upper
    middle.plane_in()
    small.out(1, small.total())
    late.plane_in()
    early.part_in()
    small.out(2, small.total())
    middle.z_in()
    late.z_in()
    early.z_in()
    small.out(3, small.total())
    middle.strip_gathered()
    early.strip_gathered()
    late.strip_gathered()
    middle.plane_gathered()
    early.plane_gathered()
    late.plane_gathered()
    small_result_ref[...] = small.total()
    early.finish()
    middle.finish()
    late.finish()


def window(*operands):
    vmem = pl.BlockSpec(memory_space=pltpu.VMEM)
    specs = [vmem] * len(operands)
    for index in (7, 8, 9, 11, 12, 14, 15, 16):
        specs[index] = pl.BlockSpec(memory_space=pltpu.HBM)
    bf16, f32 = jnp.bfloat16, jnp.float32
    return pl.pallas_call(
        window_kernel,
        name="window",
        out_shape=(
            jax.ShapeDtypeStruct((RESULT_ROWS, 128), bf16),
            jax.ShapeDtypeStruct((SMALL_ROWS, WIDTH), f32),
            jax.ShapeDtypeStruct((TOKENS, WIDTH), bf16),
        ),
        in_specs=specs,
        out_specs=(vmem, vmem, vmem),
        scratch_shapes=[
            *[pltpu.VMEM(operands[index].shape, bf16) for index in (7, 8, 9, 11, 12, 14, 15, 16)],
            pltpu.SemaphoreType.DMA((8,)),
            pltpu.VMEM((4 * HALF, 128), bf16),
            pltpu.VMEM((2 * HALF, 128), bf16),
            pltpu.VMEM((2 * HALF, 128), bf16),
            pltpu.VMEM((NEIGHBOURS * WIDTH, 128), bf16),
            pltpu.VMEM((256, NEIGHBOURS * WIDTH), bf16),
            pltpu.VMEM((3 * TOKENS, WIDTH), bf16),
            pltpu.VMEM((2, TOKENS, WIDTH), bf16),
            pltpu.VMEM((2, TOKENS, WIDTH), bf16),
            pltpu.VMEM((ROUNDS, 16, 8, 2 * WIDTH), f32),
            pltpu.VMEM((NEIGHBOURS, TOKENS, 2 * WIDTH), f32),
            pltpu.VMEM((2, ROUNDS, 24, 8, 2 * WIDTH), f32),
            pltpu.VMEM((TOKENS, 2 * WIDTH), f32),
            pltpu.VMEM((TOKENS, 2 * WIDTH), f32),
            pltpu.VMEM((TOKENS, 2 * WIDTH), f32),
            pltpu.VMEM((TOKENS, FF), bf16),
            pltpu.VMEM((TOKENS, FF), bf16),
            pltpu.VMEM((TOKENS, 3 * WIDTH), f32),
            pltpu.VMEM((TOKENS, 3 * WIDTH), bf16),
            pltpu.SemaphoreType.DMA((4,)),
            pltpu.SemaphoreType.DMA((4,)),
            *SmallSum.SCRATCH,
            *ThreeStepSum.scratch(2 * HALF),
            *TwoStepSum.scratch(HALF),
            *TwoStepSum.scratch(HALF),
        ],
        compiler_params=pltpu.CompilerParams(
            collective_id=0, has_side_effects=True, vmem_limit_bytes=36 * 2**20),
    )(*[pltpu.with_memory_space_constraint(x, pltpu.HBM) for x in operands])


def finish_kernel(scale, slabs_ref, small_ref, token_grad_in_ref, *outs):
    (token_grad_ref, flip_ref, plan_ref, gain_tanner_ref, query_ref, key_value_ref, merge_ref,
     gain_time_ref, temporal_ref, temporal_out_ref, gain_ffn_ref, up_ref, down_ref) = outs
    token_grad_ref[...] = token_grad_in_ref[...]
    small = small_ref[...] * scale
    plan_ref[...] = small[:8]
    flip_ref[...] = small[8:9]
    gain_tanner_ref[...] = small[9:10]
    gain_time_ref[...] = small[10:11]
    gain_ffn_ref[...] = small[11:12]

    def take(target, slab):
        for block in range(target.shape[0] // 256):
            for half in range(target.shape[1] // 128):
                target[block * 256 : block * 256 + 256, half * 128 : half * 128 + 128] = (
                    wide(slabs_ref[slab * 256 : slab * 256 + 256]) * scale)
                slab += 1

    take(down_ref, 0)
    take(up_ref, 8)
    take(temporal_ref, 16)
    take(temporal_out_ref, 22)
    take(query_ref, 24)
    take(key_value_ref, 26)
    take(merge_ref, 30)


def finish(scale, slabs, small, token_grad):
    vmem = pl.BlockSpec(memory_space=pltpu.VMEM)
    f32 = jnp.float32
    return pl.pallas_call(
        lambda *refs: finish_kernel(scale, *refs),
        name="finish",
        out_shape=(
            jax.ShapeDtypeStruct((TOKENS, WIDTH), jnp.bfloat16),
            jax.ShapeDtypeStruct((1, WIDTH), f32),
            jax.ShapeDtypeStruct((PLAN_STEP_COUNT, WIDTH), f32),
            jax.ShapeDtypeStruct((1, WIDTH), f32),
            jax.ShapeDtypeStruct((WIDTH, WIDTH), f32),
            jax.ShapeDtypeStruct((WIDTH, 2 * WIDTH), f32),
            jax.ShapeDtypeStruct((WIDTH, WIDTH), f32),
            jax.ShapeDtypeStruct((1, WIDTH), f32),
            jax.ShapeDtypeStruct((WIDTH, 3 * WIDTH), f32),
            jax.ShapeDtypeStruct((WIDTH, WIDTH), f32),
            jax.ShapeDtypeStruct((1, WIDTH), f32),
            jax.ShapeDtypeStruct((WIDTH, FF), f32),
            jax.ShapeDtypeStruct((FF, WIDTH), f32),
        ),
        in_specs=[vmem] * 3,
        out_specs=(vmem,) * 13,
        compiler_params=pltpu.CompilerParams(vmem_limit_bytes=32 * 2**20),
    )(slabs, small, token_grad)


def on_device(
    tokens,
    syndrome,
    check_plan_step,
    offsets,
    flip_vector,
    plan_step_embedding,
    gain_tanner,
    w_query,
    w_key_value,
    w_merge,
    gain_time,
    w_temporal,
    w_temporal_out,
    gain_ffn,
    w_ffn_up,
    w_ffn_down,
    cotangent,
):
    tile = tokens.shape
    devices = lax.axis_size("gx") * lax.axis_size("gy")
    scale = 1.0 / math.sqrt(tile[0] * tile[1] * tile[2] * devices)
    slabs, small, token_grad = window(
        tokens.reshape(TOKENS, WIDTH),
        syndrome.reshape(TOKENS // 8, 8),
        check_plan_step.reshape(TOKENS // 8, 8),
        offsets.T,
        flip_vector.reshape(1, WIDTH),
        plan_step_embedding,
        gain_tanner.reshape(1, WIDTH),
        w_query,
        w_key_value,
        w_merge,
        gain_time.reshape(1, WIDTH),
        w_temporal,
        w_temporal_out,
        gain_ffn.reshape(1, WIDTH),
        w_ffn_up,
        w_ffn_down,
        cotangent.reshape(TOKENS, WIDTH),
    )
    outs = list(finish(scale, slabs, small, token_grad))
    outs[0] = outs[0].reshape(tile)
    for index in (1, 3, 7, 10):
        outs[index] = outs[index].reshape(WIDTH)
    return tuple(outs)


def solution(mesh):
    return jax.shard_map(
        on_device,
        mesh=mesh,
        in_specs=(
            P(None, "gx", "gy", None),
            P(None, "gx", "gy"),
            P(None, "gx", "gy"),
            P(),
            P(),
            P(),
            P(),
            P(),
            P(),
            P(),
            P(),
            P(),
            P(),
            P(),
            P(),
            P(),
            P(None, "gx", "gy", None),
        ),
        out_specs=(
            P(None, "gx", "gy", None),
            P(),
            P(),
            P(),
            P(),
            P(),
            P(),
            P(),
            P(),
            P(),
            P(),
            P(),
            P(),
        ),
        check_vma=False,
    )
```
